128 devices in a mesh: col: 8 (over x_hi, z), tok: 16 (over y, x_lo, core).
Axes of the slice: x: 4 (x_hi: 2, x_lo: 2; x = x_hi * 2 + x_lo), y: 4, z: 4, core: 2. Of those that a mesh axis runs over, the one named last changes fastest.
Arguments:
- tokens_in: bfloat16 [1024, 53248], P('tok', 'col'), may hold values from -6 to 6
- codes: int32 [53248, 8192], P('col', 'tok'), may hold values from 0 to 15
- group_index: int32 [53248], P('col'), may hold values from 0 to 415
- scales: float32 [416, 8192], P(None, 'tok'), may hold values from 0.0003 to 0.002
Outputs:
- hessian_slab: float32 [512, 53248], P('col', 'tok')
- next_input: bfloat16 [1024, 8192], P('col')
The draws below stay inside these ranges and needn't reach their ends.
All inputs are finite; a program needn't handle non-finite values.
Results may differ from the reference program's by a relative error of at most 0.022.
Values may be sent and summed in bfloat16 or wider, within the bound.
A program may use at most 128 MiB of HBM per device.

```python
import math
import jax
import jax.numpy as jnp
from jax import lax

FF = 53248
DW = 8192
SLAB_DEV = 64
TOKENS = 1024
SLAB = 512
GROUPS = 416
N_COL = 8


def plant(entries, rng, least, high):
    longest = entries.shape.index(max(entries.shape))
    spots = []
    for shift in (0, 1):
        where = [jax.random.randint(jax.random.fold_in(rng, axis), (), 0, length) for axis, length in enumerate(entries.shape)]
        where[longest] = (where[longest] + shift) % entries.shape[longest]
        spots.append(tuple(where))
    return entries.at[spots[0]].set(least).at[spots[1]].set(high)


def shard_levels(rng, dims, shards, low, largest):
    level = 1.0
    for axis_at, blocks in shards:
        draws = jax.random.uniform(jax.random.fold_in(jax.random.fold_in(rng, 6), axis_at), (blocks,), jnp.float32, low / len(shards), largest / len(shards))
        level = level * jnp.repeat(jnp.exp(draws), dims[axis_at] // blocks).reshape((-1,) + (1,) * (len(dims) - 1 - axis_at))
    return level


def noise(own_key, shape, spread, bound, cuts=(), kind=jnp.bfloat16):
    level = shard_levels(own_key, shape, cuts, -0.22, 0.18) if cuts else 1.0
    entries = jax.random.normal(own_key, shape, jnp.float32) * spread * level
    return jnp.minimum(jnp.maximum(entries, -bound), bound).astype(kind)


def setup_inputs(seed: int = 0) -> dict:
    keys = jax.random.split(jax.random.key(seed), 5)
    return {
        "tokens_in": noise(keys[0], (TOKENS, FF), 1.0, 6.0, ((0, 16), (1, 8))),
        "codes": plant(jax.random.randint(keys[1], (FF, DW), 0, 16), jax.random.fold_in(keys[1], 1), 0, 15).astype(jnp.int32),
        "group_index": plant(jax.random.randint(keys[2], (FF,), 0, GROUPS), jax.random.fold_in(keys[2], 1), 0, GROUPS - 1).astype(jnp.int32),
        "scales": jnp.clip(jnp.exp(math.log(0.002) - 1.89712 * jax.random.uniform(keys[3], (GROUPS, DW), jnp.float32) ** shard_levels(keys[3], (GROUPS, DW), ((1, 16),), -0.2, 0.2)), 0.0003, 0.002),
    }


def reference(tokens_in, codes, group_index, scales):
    panel_width = FF // N_COL
    slab_input = tokens_in.reshape(TOKENS, N_COL, panel_width)[:, :, :SLAB_DEV].reshape(TOKENS, SLAB)
    hessian_slab = jnp.dot(slab_input.T, tokens_in, preferred_element_type=jnp.float32) * (2.0 / TOKENS)

    def one_panel(running, panel_index):
        first_col = (panel_index * panel_width).astype(jnp.int32)
        code_rows = lax.dynamic_slice_in_dim(codes, first_col, panel_width, 0)
        groups = lax.dynamic_slice_in_dim(group_index, first_col, panel_width, 0)
        weights = (jnp.take(scales, groups, axis=0) * (code_rows - 8).astype(jnp.float32)).astype(jnp.bfloat16)
        inputs = lax.dynamic_slice_in_dim(tokens_in, first_col, panel_width, 1)
        return running + jnp.dot(inputs, weights, preferred_element_type=jnp.float32), None

    running, unused = lax.scan(one_panel, jnp.zeros((TOKENS, DW), jnp.float32), jnp.arange(N_COL, dtype=jnp.int32))
    return hessian_slab, running.astype(jnp.bfloat16)
```

```python
import jax
import jax.numpy as jnp
from jax import lax
from jax.experimental import pallas as pl
from jax.experimental.pallas import tpu as pltpu
from jax.sharding import PartitionSpec as P

MESH = pl.DeviceIdType.MESH
SLAB_DEV = 64
LANES = 128
NC = 4
X1, YP, YM, Y2, YPX, YMX, X2, OWN = range(8)


def kernel(
    x_hbm, codes_hbm, gi_hbm, scales_hbm, out_ref, hes_ref,
    xbuf, wbuf, codes, gi, scales, hi, mid, lo, oh, pbuf, rbuf, slab, hs, acc,
    lsem, csem, line_s, line_r, sib_s, sib_r, slab_s, slab_r, d_s, d_r, e_s, e_r, es_s, es_r, h_s, h_r,
):
    c = lax.axis_index("col")
    t = lax.axis_index("tok")
    y, x, q = t // 4, (t // 2) % 2, t % 2
    k_slab, h_half = t // 2, t % 2
    rows, width = x_hbm.shape
    cw = width // NC
    half = width // 2
    n_blk = csem.shape[0]
    blk = width // n_blk
    dcols = out_ref.shape[1] // 16
    groups = scales.shape[0]

    def slot(dy, dx):
        return ((y + dy) % 4) * 4 + ((x + dx) % 2) * 2 + q

    def sibling(s):
        return s + 1 - 2 * (s % 2)

    yp, ym, xn, sib = slot(1, 0), slot(3, 0), slot(0, 1), sibling(t)
    part = 2 * c + h_half

    own = pltpu.make_async_copy(x_hbm, xbuf.at[t], lsem.at[0])
    own.start()
    gi_cp = pltpu.make_async_copy(gi_hbm, gi, lsem.at[1])
    gi_cp.start()
    sc_cp = pltpu.make_async_copy(scales_hbm, scales, lsem.at[2])
    sc_cp.start()

    def code_copy(b):
        r = pl.ds(pl.multiple_of(b * blk, blk), blk)
        return pltpu.make_async_copy(codes_hbm.at[r], codes.at[r], csem.at[b])

    @pl.loop(0, n_blk)
    def _(b):
        code_copy(b).start()

    bar = pltpu.get_barrier_semaphore()

    def greet(cc, tt):
        pl.semaphore_signal(bar, inc=1, device_id=(cc, tt), device_id_type=MESH)

    for dy in range(4):
        for dx in range(2):
            if dy or dx:
                greet(c, slot(dy, dx))
    greet(c, sib)

    @pl.loop(1, 8)
    def _(d):
        greet((c + d) % 8, t)

    @pl.when(k_slab != c)
    def _():
        greet(k_slab, part)

        @pl.loop(0, 16)
        def _(i):
            greet(k_slab, i)

        pl.semaphore_wait(bar, 8 + 7 + 1 + 16)

    @pl.when(k_slab == c)
    def _():
        @pl.loop(1, 16)
        def _(d):
            greet(k_slab, (t + d) % 16)

        pl.semaphore_wait(bar, 8 + 7 + 15)

    def cols(ch):
        return pl.ds(ch * cw, cw)

    def line(kind, tag, ch, s, dev, src=None):
        src = xbuf.at[s] if src is None else src
        return pltpu.make_async_remote_copy(
            src_ref=src.at[:, cols(ch)], dst_ref=xbuf.at[s, :, cols(ch)],
            send_sem=line_s.at[tag, ch], recv_sem=line_r.at[kind, ch],
            device_id=(c, dev), device_id_type=MESH,
        )

    def across(kind, ch, s, src=None):
        src = xbuf.at[s] if src is None else src
        return pltpu.make_async_remote_copy(
            src_ref=src.at[:, cols(ch)], dst_ref=xbuf.at[s, :, cols(ch)],
            send_sem=sib_s.at[kind, ch], recv_sem=sib_r.at[kind, ch],
            device_id=(c, sib), device_id_type=MESH,
        )

    slots = {
        X1: slot(0, 1), YP: slot(3, 0), YM: slot(1, 0), Y2: slot(2, 0),
        YPX: slot(3, 1), YMX: slot(1, 1), X2: slot(2, 1), OWN: t,
    }

    def got(kind, ch):
        line(kind, kind, ch, slots[kind], yp).wait_recv()

    def got_sib(kind):
        s = sibling(slots[kind])
        for ch in range(NC):
            across(kind, ch, s).wait_recv()

    for ch in range(NC):
        line(YP, YP, ch, t, yp, x_hbm).start()
        line(YM, YM, ch, t, ym, x_hbm).start()
        line(X1, X1, ch, t, xn, x_hbm).start()
    for ch in range(NC):
        across(OWN, ch, t, x_hbm).start()

    def slab_copy(cc, tt, i):
        return pltpu.make_async_remote_copy(
            src_ref=x_hbm.at[:, pl.ds(0, LANES)], dst_ref=slab.at[t],
            send_sem=slab_s.at[i], recv_sem=slab_r.at[t],
            device_id=(cc, tt), device_id_type=MESH,
        )

    def to_slab_users(act):
        @pl.loop(0, 16)
        def _(i):
            cc, tt = i // 2, 2 * c + i % 2

            @pl.when(jnp.logical_or(cc != c, tt != t))
            def _():
                act(slab_copy(cc, tt, i))

    sc_cp.wait()
    gi_cp.wait()
    for ref in (hi, mid, lo):
        ref[pl.ds(groups - groups % 32, 512 - groups + groups % 32), :] = jnp.zeros(
            (512 - groups + groups % 32, dcols), jnp.bfloat16
        )

    @pl.loop(0, groups // 32)
    def _(i):
        r = pl.ds(pl.multiple_of(i * 32, 32), 32)
        s = scales[r, :]
        a = s.astype(jnp.bfloat16)
        rest = s - a.astype(jnp.float32)
        b = rest.astype(jnp.bfloat16)
        hi[r, :] = a
        mid[r, :] = b
        lo[r, :] = (rest - b.astype(jnp.float32)).astype(jnp.bfloat16)

    own.wait()

    def dequant(b):
        code_copy(b).wait()
        ids = lax.broadcasted_iota(jnp.int32, (LANES, 512), 1).astype(jnp.float32)
        for r in range(blk // LANES):
            g = gi[pl.ds(b * (blk // LANES) + r, 1), :].astype(jnp.float32)
            g = jnp.transpose(jnp.broadcast_to(g, (LANES, LANES)))
            g = jnp.concatenate([g] * 4, axis=1)
            oh[pl.ds(r * LANES, LANES), :] = jnp.where(g == ids, 1.0, 0.0).astype(jnp.bfloat16)
        one = oh[...]
        s = (
            jnp.dot(one, hi[...], preferred_element_type=jnp.float32)
            + jnp.dot(one, mid[...], preferred_element_type=jnp.float32)
            + jnp.dot(one, lo[...], preferred_element_type=jnp.float32)
        )
        r = pl.ds(pl.multiple_of(b * blk, blk), blk)
        wbuf[r, :] = (s * (codes[r, :].astype(jnp.float32) - 8.0)).astype(jnp.bfloat16)

    @pl.loop(0, n_blk)
    def _(b):
        dequant(b)

    to_slab_users(lambda cp: cp.start())

    def product(k, lo_ch, n_ch, first):
        @pl.loop(lo_ch, lo_ch + n_ch)
        def _(ch):
            r = pl.ds(pl.multiple_of(ch * cw, LANES), cw)
            a = xbuf[pl.ds(2 * k, 2), :, r].reshape(2 * rows, cw)
            p = jnp.dot(a, wbuf[r, :], preferred_element_type=jnp.float32)

            if first:
                @pl.when(ch == lo_ch)
                def _():
                    acc[...] = p

                @pl.when(ch != lo_ch)
                def _():
                    acc[...] += p
            else:
                acc[...] += p

    def d_copy(k):
        return pltpu.make_async_remote_copy(
            src_ref=pbuf.at[k], dst_ref=rbuf.at[c],
            send_sem=d_s.at[k], recv_sem=d_r.at[c],
            device_id=(k, t), device_id_type=MESH,
        )

    def finish(kind):
        s = slots[kind]
        got_sib(kind)
        k = s // 2
        product(k, 0, NC, True)

        @pl.when(k == c)
        def _():
            rbuf[c] = acc[...].astype(jnp.bfloat16)

        @pl.when(k != c)
        def _():
            pbuf[k] = acc[...].astype(jnp.bfloat16)
            d_copy(k).start()

    for ch in range(NC):
        got(YP, ch)
        got(YM, ch)
        if ch < NC // 2:
            line(Y2, Y2, ch, slots[YP], yp).start()
        else:
            line(Y2, Y2, ch, slots[YM], ym).start()
        across(YP, ch, slots[YP]).start()
        across(YM, ch, slots[YM]).start()
    for ch in range(NC):
        got(X1, ch)
        across(X1, ch, slots[X1]).start()
    finish(OWN)
    finish(X1)
    for ch in range(NC):
        line(Y2, Y2, ch, slots[YP], yp).wait_send()
        line(YPX, YPX, ch, slots[X1], yp).start()
        line(YMX, YMX, ch, slots[X1], ym).start()
    for ch in range(NC):
        got(Y2, ch)
        line(X2, X2, ch, slots[Y2], xn).start()
        across(Y2, ch, slots[Y2]).start()
    finish(YP)
    finish(YM)
    finish(Y2)
    for ch in range(NC):
        for kind in (YPX, YMX, X2):
            got(kind, ch)
            across(kind, ch, slots[kind]).start()
    finish(YPX)
    finish(YMX)
    finish(X2)

    @pl.loop(0, 16)
    def _(i):
        @pl.when(jnp.logical_or(k_slab != c, i != t))
        def _():
            pltpu.make_async_remote_copy(
                src_ref=slab.at[i], dst_ref=slab.at[i],
                send_sem=slab_s.at[i], recv_sem=slab_r.at[i],
                device_id=(c, sib), device_id_type=MESH,
            ).wait_recv()

    @pl.when(k_slab == c)
    def _():
        slab[t] = xbuf[t, :, pl.ds(0, LANES)]

    st = jnp.transpose(slab[...].reshape(16 * rows, LANES).astype(jnp.float32))
    st = st[:SLAB_DEV].astype(jnp.bfloat16)

    @pl.loop(0, half // 256)
    def _(j):
        src = pl.ds(pl.multiple_of(h_half * half + j * 256, 256), 256)
        a = xbuf[:, :, src].reshape(16 * rows, 256)
        hs[:, pl.ds(pl.multiple_of(j * 256, 256), 256)] = jnp.dot(
            st, a, preferred_element_type=jnp.float32
        ).astype(jnp.bfloat16)

    h_copy = pltpu.make_async_remote_copy(
        src_ref=hs, dst_ref=hes_ref, send_sem=h_s, recv_sem=h_r,
        device_id=(k_slab, part), device_id_type=MESH,
    )

    @pl.when(k_slab != c)
    def _():
        h_copy.start()

    @pl.when(k_slab == c)
    def _():
        hes_ref[...] = hs[...]

    @pl.loop(1, 8)
    def _(d):
        s = (c + d) % 8
        pltpu.make_async_remote_copy(
            src_ref=pbuf.at[s], dst_ref=rbuf.at[s], send_sem=d_s.at[s], recv_sem=d_r.at[s],
            device_id=(s, t), device_id_type=MESH,
        ).wait_recv()

    def out_cols(s):
        return pl.ds(pl.multiple_of(s * dcols, dcols), dcols)

    acc[...] = rbuf[0].astype(jnp.float32)

    @pl.loop(1, 8)
    def _(i):
        acc[...] += rbuf[i].astype(jnp.float32)

    out_ref[:, out_cols(t)] = acc[...].astype(jnp.bfloat16)

    def e_copy(s, d, dev):
        return pltpu.make_async_remote_copy(
            src_ref=out_ref.at[:, out_cols(s)], dst_ref=out_ref.at[:, out_cols(s)],
            send_sem=e_s.at[d], recv_sem=e_r.at[d],
            device_id=(c, dev), device_id_type=MESH,
        )

    def es_copy(s, d):
        return pltpu.make_async_remote_copy(
            src_ref=out_ref.at[:, out_cols(s)], dst_ref=out_ref.at[:, out_cols(s)],
            send_sem=es_s.at[d], recv_sem=es_r.at[d],
            device_id=(c, sib), device_id_type=MESH,
        )

    others = [(2, 0), (2, 1), (1, 0), (3, 0), (1, 1), (3, 1), (0, 1)]
    for dy, dx in others:
        e_copy(t, 2 * dy + dx, slot(dy, dx)).start()
    es_copy(t, 0).start()
    for dy, dx in reversed(others):
        s = slot(-dy % 4, dx)
        e_copy(s, 2 * dy + dx, sib).wait_recv()
        es_copy(s, 2 * dy + dx).start()
    for d in range(8):
        s = slot(-(d // 2) % 4, d % 2)
        es_copy(sibling(s), d).wait_recv()

    @pl.when(k_slab != c)
    def _():
        h_copy.wait_send()
        h_copy.wait_recv()

    for d in range(8):
        es_copy(t, d).wait_send()
        if d:
            e_copy(t, d, sib).wait_send()

    @pl.loop(1, 8)
    def _(d):
        d_copy((c + d) % 8).wait_send()

    to_slab_users(lambda cp: cp.wait_send())
    for kind in range(8):
        for ch in range(NC):
            if kind not in (Y2, OWN):
                line(kind, kind, ch, t, yp).wait_send()
            across(kind, ch, t).wait_send()


def fused(tokens_in, codes, group_index, scales):
    rows, width = tokens_in.shape
    dcols = codes.shape[1]
    bf, f32 = jnp.bfloat16, jnp.float32
    dma = pltpu.SemaphoreType.DMA
    n_blk = 13
    return pl.pallas_call(
        kernel,
        name="calibrate",
        out_shape=(
            jax.ShapeDtypeStruct((128, 16 * dcols), bf),
            jax.ShapeDtypeStruct((SLAB_DEV, width // 2), bf),
        ),
        in_specs=[pl.BlockSpec(memory_space=pl.ANY)] * 4,
        out_specs=[pl.BlockSpec(memory_space=pltpu.VMEM)] * 2,
        scratch_shapes=[
            pltpu.VMEM((16, rows, width), bf),
            pltpu.VMEM((width, dcols), bf),
            pltpu.VMEM((width, dcols), jnp.int32),
            pltpu.VMEM((width // LANES, LANES), jnp.int32),
            pltpu.VMEM(scales.shape, f32),
            pltpu.VMEM((512, dcols), bf),
            pltpu.VMEM((512, dcols), bf),
            pltpu.VMEM((512, dcols), bf),
            pltpu.VMEM((width // n_blk, 512), bf),
            pltpu.VMEM((8, 2 * rows, dcols), bf),
            pltpu.VMEM((8, 2 * rows, dcols), bf),
            pltpu.VMEM((16, rows, LANES), bf),
            pltpu.VMEM((SLAB_DEV, width // 2), bf),
            pltpu.VMEM((2 * rows, dcols), f32),
            dma((3,)), dma((n_blk,)),
            dma((8, NC)), dma((8, NC)), dma((8, NC)), dma((8, NC)),
            dma((16,)), dma((16,)), dma((8,)), dma((8,)),
            dma((8,)), dma((8,)), dma((8,)), dma((8,)),
            dma, dma,
        ],
        compiler_params=pltpu.CompilerParams(
            collective_id=0, has_side_effects=True, vmem_limit_bytes=60 << 20
        ),
        cost_estimate=pl.CostEstimate(
            flops=16 * 10**9, bytes_accessed=20 * 10**6, transcendentals=0
        ),
    )(tokens_in, codes, group_index.reshape(width // LANES, LANES), scales)


def local(tokens_in, codes, group_index, scales):
    total_tokens = tokens_in.shape[0] * lax.axis_size("tok")
    next_input, hessian = fused(tokens_in, codes, group_index, scales)
    return hessian.astype(jnp.float32) * (2.0 / total_tokens), next_input


def solution(mesh):
    return jax.shard_map(
        local,
        mesh=mesh,
        in_specs=(P("tok", "col"), P("col", "tok"), P("col"), P(None, "tok")),
        out_specs=(P("col", "tok"), P("col", None)),
        check_vma=False,
    )
```

```python
import jax
import jax.numpy as jnp
from jax import lax
from jax.experimental import pallas as pl
from jax.experimental.pallas import tpu as pltpu
from jax.sharding import PartitionSpec as P

MESH = pl.DeviceIdType.MESH
SLAB_DEV = 64
LANES = 128
CW = 512
N_DATA = 13
NJ = 14
SLAB_J = 5
X1, YP, YM, Y2, YPX, YMX, X2, OWN = range(8)


def kernel(
    x_hbm, codes_hbm, gi_hbm, scales_hbm, out_ref, hes_ref,
    xbuf, wbuf, codes, gi, scales, hi, mid, lo, oh, pbuf, rbuf, slab, st, hs, h1, acc,
    lsem, csem, line_s, line_r, sib_s, sib_r, slab_s, slab_r, d_s, d_r, e_s, e_r, es_s, es_r,
    h1_s, h1_r, h2_s, h2_r,
):
    c = lax.axis_index("col")
    t = lax.axis_index("tok")
    y, x, q = t // 4, (t // 2) % 2, t % 2
    p = t // 2
    rows, width = x_hbm.shape
    half = width // 2
    dcols = out_ref.shape[1] // 16
    groups = scales.shape[0]

    def slot(dy, dx):
        return ((y + dy) % 4) * 4 + ((x + dx) % 2) * 2 + q

    def sibling(s):
        return s + 1 - 2 * (s % 2)

    yp, ym, xn, sib = slot(1, 0), slot(3, 0), slot(0, 1), sibling(t)

    own = pltpu.make_async_copy(x_hbm, xbuf.at[t, :, pl.ds(0, width)], lsem.at[0])
    own.start()
    own_slab = pltpu.make_async_copy(x_hbm.at[:, pl.ds(0, LANES)], slab.at[c], lsem.at[3])
    own_slab.start()
    gi_cp = pltpu.make_async_copy(gi_hbm, gi, lsem.at[1])
    gi_cp.start()
    sc_cp = pltpu.make_async_copy(scales_hbm, scales, lsem.at[2])
    sc_cp.start()

    def code_copy(b):
        r = pl.ds(pl.multiple_of(b * CW, CW), CW)
        return pltpu.make_async_copy(codes_hbm.at[r], codes.at[r], csem.at[b])

    @pl.loop(0, N_DATA)
    def _(b):
        code_copy(b).start()

    bar = pltpu.get_barrier_semaphore()

    def greet(cc, tt):
        pl.semaphore_signal(bar, inc=1, device_id=(cc, tt), device_id_type=MESH)

    for dy in range(4):
        for dx in range(2):
            if dy or dx:
                greet(c, slot(dy, dx))
    greet(c, sib)

    @pl.loop(1, 8)
    def _(d):
        greet((c + d) % 8, t)

    pl.semaphore_wait(bar, 15)

    def slab_copy(d):
        return pltpu.make_async_remote_copy(
            src_ref=x_hbm.at[:, pl.ds(0, LANES)], dst_ref=slab.at[c],
            send_sem=slab_s.at[d], recv_sem=slab_r.at[d],
            device_id=((c + d) % 8, t), device_id_type=MESH,
        )

    @pl.loop(1, 8)
    def _(d):
        slab_copy(d).start()

    def col0(j):
        s = j - jnp.where(j > SLAB_J, 1, 0)
        chunk = jnp.where(j == SLAB_J, N_DATA, s // 2 + 7 * (s % 2))
        return pl.multiple_of(chunk * CW, CW)

    def line(kind, j, s, dev, src=None):
        cols = pl.ds(col0(j), CW)
        src = xbuf.at[s] if src is None else src
        return pltpu.make_async_remote_copy(
            src_ref=src.at[:, cols], dst_ref=xbuf.at[s, :, cols],
            send_sem=line_s.at[kind, j], recv_sem=line_r.at[kind, j],
            device_id=(c, dev), device_id_type=MESH,
        )

    def across(kind, j, s, src=None):
        cols = pl.ds(col0(j), CW)
        src = xbuf.at[s] if src is None else src
        return pltpu.make_async_remote_copy(
            src_ref=src.at[:, cols], dst_ref=xbuf.at[s, :, cols],
            send_sem=sib_s.at[kind, j], recv_sem=sib_r.at[kind, j],
            device_id=(c, sib), device_id_type=MESH,
        )

    slots = {
        X1: slot(0, 1), YP: slot(3, 0), YM: slot(1, 0), Y2: slot(2, 0),
        YPX: slot(3, 1), YMX: slot(1, 1), X2: slot(2, 1), OWN: t,
    }

    def got(kind, j):
        line(kind, j, slots[kind], yp).wait_recv()

    def got_sib(kind, j):
        across(kind, j, sibling(slots[kind])).wait_recv()

    def send_own(j, src):
        line(YP, j, t, yp, src).start()
        line(YM, j, t, ym, src).start()
        line(X1, j, t, xn, src).start()
        across(OWN, j, t, src).start()

    @pl.loop(0, SLAB_J)
    def _(j):
        send_own(j, x_hbm)

    sc_cp.wait()
    gi_cp.wait()
    for ref in (hi, mid, lo):
        ref[pl.ds(groups, 512 - groups), :] = jnp.zeros((512 - groups, dcols), jnp.bfloat16)

    @pl.loop(0, groups // 32)
    def _(i):
        r = pl.ds(pl.multiple_of(i * 32, 32), 32)
        s = scales[r, :]
        a = s.astype(jnp.bfloat16)
        rest = s - a.astype(jnp.float32)
        b = rest.astype(jnp.bfloat16)
        hi[r, :] = a
        mid[r, :] = b
        lo[r, :] = (rest - b.astype(jnp.float32)).astype(jnp.bfloat16)

    def dequant(b):
        code_copy(b).wait()
        ids = lax.broadcasted_iota(jnp.int32, (LANES, 512), 1).astype(jnp.float32)
        for r in range(CW // LANES):
            g = gi[pl.ds(b * (CW // LANES) + r, 1), :].astype(jnp.float32)
            g = jnp.transpose(jnp.broadcast_to(g, (LANES, LANES)))
            g = jnp.concatenate([g] * 4, axis=1)
            oh[pl.ds(r * LANES, LANES), :] = jnp.where(g == ids, 1.0, 0.0).astype(jnp.bfloat16)
        one = oh[...]
        s = (
            jnp.dot(one, hi[...], preferred_element_type=jnp.float32)
            + jnp.dot(one, mid[...], preferred_element_type=jnp.float32)
            + jnp.dot(one, lo[...], preferred_element_type=jnp.float32)
        )
        r = pl.ds(pl.multiple_of(b * CW, CW), CW)
        wbuf[r, :] = (s * (codes[r, :].astype(jnp.float32) - 8.0)).astype(jnp.bfloat16)

    own_slab.wait()

    @pl.loop(1, 8)
    def _(d):
        slab_copy(d).wait_recv()

    for i in range(4):
        pair = jnp.concatenate([slab[2 * i][:, :SLAB_DEV], slab[2 * i + 1][:, :SLAB_DEV]], axis=1)
        xbuf[t, :, pl.ds(width + i * LANES, LANES)] = pair
    send_own(SLAB_J, xbuf.at[t])

    @pl.loop(SLAB_J + 1, NJ)
    def _(j):
        send_own(j, x_hbm)

    own.wait()

    @pl.loop(0, NJ)
    def _(j):
        @pl.when(j < N_DATA)
        def _():
            dequant(j)

        got(YP, j)
        got(YM, j)

        @pl.when(j % 2 == 0)
        def _():
            line(Y2, j, slots[YP], yp).start()

        @pl.when(j % 2 == 1)
        def _():
            line(Y2, j, slots[YM], ym).start()

        across(YP, j, slots[YP]).start()
        across(YM, j, slots[YM]).start()
        got(X1, j)
        across(X1, j, slots[X1]).start()

    @pl.loop(0, NJ)
    def _(j):
        line(YPX, j, slots[X1], yp).start()
        line(YMX, j, slots[X1], ym).start()

    def chunk_product(kinds, j):
        @pl.when(j != SLAB_J)
        def _():
            r = pl.ds(col0(j), CW)
            a = jnp.concatenate(
                [xbuf[pl.ds(2 * (slots[k] // 2), 2), :, r].reshape(2 * rows, CW) for k in kinds], axis=0
            )
            prod = jnp.dot(a, wbuf[r, :], preferred_element_type=jnp.float32)
            acc[pl.ds(0, len(kinds))] += prod.reshape(len(kinds), 2 * rows, dcols)

    def d_copy(k):
        return pltpu.make_async_remote_copy(
            src_ref=pbuf.at[k], dst_ref=rbuf.at[c],
            send_sem=d_s.at[k], recv_sem=d_r.at[c],
            device_id=(k, t), device_id_type=MESH,
        )

    def send_terms(kinds):
        for i, kind in enumerate(kinds):
            k = slots[kind] // 2

            @pl.when(k == c)
            def _():
                rbuf[c] = acc[i].astype(jnp.bfloat16)

            @pl.when(k != c)
            def _():
                pbuf[k] = acc[i].astype(jnp.bfloat16)
                d_copy(k).start()

    near = (OWN, X1, YP, YM)
    acc[...] = jnp.zeros_like(acc)

    @pl.loop(0, NJ)
    def _(j):
        got(Y2, j)
        line(X2, j, slots[Y2], xn).start()
        across(Y2, j, slots[Y2]).start()
        for kind in near:
            got_sib(kind, j)
        chunk_product(near, j)

    send_terms(near)
    acc[...] = jnp.zeros_like(acc)

    @pl.loop(0, NJ)
    def _(j):
        got_sib(Y2, j)
        chunk_product((Y2,), j)

    send_terms((Y2,))
    acc[...] = jnp.zeros_like(acc)

    def out_cols(s):
        return pl.ds(pl.multiple_of(s * dcols, dcols), dcols)

    def e_copy(s, d, dev):
        return pltpu.make_async_remote_copy(
            src_ref=out_ref.at[:, out_cols(s)], dst_ref=out_ref.at[:, out_cols(s)],
            send_sem=e_s.at[d], recv_sem=e_r.at[d],
            device_id=(c, dev), device_id_type=MESH,
        )

    def es_copy(s, d):
        return pltpu.make_async_remote_copy(
            src_ref=out_ref.at[:, out_cols(s)], dst_ref=out_ref.at[:, out_cols(s)],
            send_sem=es_s.at[d], recv_sem=es_r.at[d],
            device_id=(c, sib), device_id_type=MESH,
        )

    others = [(2, 0), (2, 1), (1, 0), (3, 0), (1, 1), (3, 1), (0, 1)]

    def total_and_share():
        @pl.loop(1, 8)
        def _(d):
            s = (c + d) % 8
            pltpu.make_async_remote_copy(
                src_ref=pbuf.at[s], dst_ref=rbuf.at[s], send_sem=d_s.at[s], recv_sem=d_r.at[s],
                device_id=(s, t), device_id_type=MESH,
            ).wait_recv()

        total = rbuf[0].astype(jnp.float32)
        for i in range(1, 8):
            total += rbuf[i].astype(jnp.float32)
        out_ref[:, out_cols(t)] = total.astype(jnp.bfloat16)
        for dy, dx in others:
            e_copy(t, 2 * dy + dx, slot(dy, dx)).start()
        es_copy(t, 0).start()

    wide = p % 4 == 0
    first = 3 * p + (p + 7) // 8 + (p + 3) // 8
    ready = jnp.where(p == 0, jnp.where(q == 1, NJ - 1, SLAB_J + 2), jnp.minimum(2 * p + 1, NJ - 1))
    ready = jnp.maximum(ready, SLAB_J + 2)

    def h_part(off, n):
        src = pl.ds(pl.multiple_of(q * half + (first + off) * LANES, LANES), n * LANES)
        a = xbuf[:, :, src].reshape(16 * rows, n * LANES)
        r = jnp.dot(st[...], a, preferred_element_type=jnp.float32)
        hs[:, :, pl.ds(off * LANES, n * LANES)] = r.astype(jnp.bfloat16).reshape(8, SLAB_DEV, n * LANES)

    def h1_copy(k, n):
        cols = pl.ds(0, n * LANES)
        return pltpu.make_async_remote_copy(
            src_ref=hs.at[k, :, cols], dst_ref=h1.at[c, :, cols],
            send_sem=h1_s.at[k], recv_sem=h1_r.at[c],
            device_id=(k, t), device_id_type=MESH,
        )

    def h1_wait(s, n):
        cols = pl.ds(0, n * LANES)
        pltpu.make_async_remote_copy(
            src_ref=hs.at[s, :, cols], dst_ref=h1.at[s, :, cols],
            send_sem=h1_s.at[s], recv_sem=h1_r.at[s],
            device_id=(s, t), device_id_type=MESH,
        ).wait_recv()

    def either(f):
        @pl.when(wide)
        def _():
            f(4)

        @pl.when(jnp.logical_not(wide))
        def _():
            f(3)

    def hessian():
        h_part(0, 3)

        @pl.when(wide)
        def _():
            h_part(3, 1)

        h1[c] = hs[c]

        @pl.loop(1, 8)
        def _(d):
            either(lambda n: h1_copy((c + d) % 8, n).start())

    far = (YPX, YMX, X2)

    def third(j):
        @pl.when(j < NJ)
        def _():
            for kind in far:
                got(kind, j)
                across(kind, j, slots[kind]).start()

        @pl.when(j > 0)
        def _():
            for kind in far:
                got_sib(kind, j - 1)
            chunk_product(far, j - 1)

            @pl.when(j - 1 == ready)
            def _():
                hessian()

    @pl.loop(0, SLAB_J + 2)
    def _(j):
        third(j)

    @pl.loop(0, 4)
    def _(i):
        src = pl.ds(pl.multiple_of(width + i * LANES, LANES), LANES)
        a = xbuf[:, :, src].reshape(16 * rows, LANES).astype(jnp.float32)
        st[pl.ds(pl.multiple_of(i * LANES, LANES), LANES), :] = jnp.transpose(a).astype(jnp.bfloat16)

    early = jnp.logical_or(c % 2 == x, c // 2 == y)

    @pl.when(early)
    def _():
        total_and_share()

    @pl.loop(SLAB_J + 2, NJ + 1)
    def _(j):
        third(j)

    send_terms(far)

    def place(s):
        return 2 * s + q

    def h2_copy(s, n):
        dst = hes_ref.at[:, pl.ds(pl.multiple_of(first * LANES, LANES), n * LANES)]
        return pltpu.make_async_remote_copy(
            src_ref=h1.at[s, :, pl.ds(0, n * LANES)], dst_ref=dst,
            send_sem=h2_s.at[s], recv_sem=h2_r.at[p],
            device_id=(c, place(s)), device_id_type=MESH,
        )

    def h2_wait(s, n):
        f = 3 * s + (s + 7) // 8 + (s + 3) // 8
        dst = hes_ref.at[:, pl.ds(pl.multiple_of(f * LANES, LANES), n * LANES)]
        pltpu.make_async_remote_copy(
            src_ref=h1.at[s, :, pl.ds(0, n * LANES)], dst_ref=dst,
            send_sem=h2_s.at[s], recv_sem=h2_r.at[s],
            device_id=(c, place(s)), device_id_type=MESH,
        ).wait_recv()

    @pl.loop(1, 8)
    def _(d):
        either(lambda n: h1_wait((c + d) % 8, n))

    @pl.loop(1, 8)
    def _(d):
        either(lambda n: h2_copy((p + d) % 8, n).start())

    def keep(n):
        hes_ref[:, pl.ds(pl.multiple_of(first * LANES, LANES), n * LANES)] = h1[p, :, pl.ds(0, n * LANES)]

    either(keep)

    @pl.when(jnp.logical_not(early))
    def _():
        total_and_share()

    for dy, dx in reversed(others):
        s = slot(-dy % 4, dx)
        e_copy(s, 2 * dy + dx, sib).wait_recv()
        es_copy(s, 2 * dy + dx).start()
    for d in range(8):
        s = slot(-(d // 2) % 4, d % 2)
        es_copy(sibling(s), d).wait_recv()

    for s in range(8):
        @pl.when(s != p)
        def _():
            h2_wait(s, 4 if s % 4 == 0 else 3)

    @pl.loop(1, 8)
    def _(d):
        either(lambda n: h1_copy((c + d) % 8, n).wait_send())
        either(lambda n: h2_copy((p + d) % 8, n).wait_send())
        d_copy((c + d) % 8).wait_send()
        slab_copy(d).wait_send()

    for d in range(8):
        es_copy(t, d).wait_send()
        if d:
            e_copy(t, d, sib).wait_send()

    @pl.loop(0, NJ)
    def _(j):
        for kind in range(8):
            if kind != OWN:
                line(kind, j, t, yp).wait_send()
            across(kind, j, t).wait_send()


def fused(tokens_in, codes, group_index, scales):
    rows, width = tokens_in.shape
    dcols = codes.shape[1]
    bf, f32 = jnp.bfloat16, jnp.float32
    dma = pltpu.SemaphoreType.DMA
    table = pltpu.VMEM((512, dcols), bf)
    return pl.pallas_call(
        kernel,
        name="calibrate",
        out_shape=(
            jax.ShapeDtypeStruct((128, 16 * dcols), bf),
            jax.ShapeDtypeStruct((SLAB_DEV, width // 2), bf),
        ),
        in_specs=[pl.BlockSpec(memory_space=pl.ANY)] * 4,
        out_specs=[pl.BlockSpec(memory_space=pltpu.VMEM)] * 2,
        scratch_shapes=[
            pltpu.VMEM((16, rows, width + CW), bf),
            pltpu.VMEM((width, dcols), bf),
            pltpu.VMEM((width, dcols), jnp.int32),
            pltpu.VMEM((width // LANES, LANES), jnp.int32),
            pltpu.VMEM(scales.shape, f32),
            table, table, table,
            pltpu.VMEM((CW, 512), bf),
            pltpu.VMEM((8, 2 * rows, dcols), bf),
            pltpu.VMEM((8, 2 * rows, dcols), bf),
            pltpu.VMEM((8, rows, LANES), bf),
            pltpu.VMEM((512, 16 * rows), bf),
            pltpu.VMEM((8, SLAB_DEV, 512), bf),
            pltpu.VMEM((8, SLAB_DEV, 512), bf),
            pltpu.VMEM((4, 2 * rows, dcols), f32),
            dma((4,)), dma((N_DATA,)),
            dma((8, NJ)), dma((8, NJ)), dma((8, NJ)), dma((8, NJ)),
            dma((8,)), dma((8,)), dma((8,)), dma((8,)),
            dma((8,)), dma((8,)), dma((8,)), dma((8,)),
            dma((8,)), dma((8,)), dma((8,)), dma((8,)),
        ],
        compiler_params=pltpu.CompilerParams(
            collective_id=0, has_side_effects=True, vmem_limit_bytes=60 << 20
        ),
        cost_estimate=pl.CostEstimate(
            flops=16 * 10**9, bytes_accessed=20 * 10**6, transcendentals=0
        ),
    )(tokens_in, codes, group_index.reshape(width // LANES, LANES), scales)


def local(tokens_in, codes, group_index, scales):
    total_tokens = tokens_in.shape[0] * lax.axis_size("tok")
    next_input, hessian = fused(tokens_in, codes, group_index, scales)
    return hessian.astype(jnp.float32) * (2.0 / total_tokens), next_input


def solution(mesh):
    return jax.shard_map(
        local,
        mesh=mesh,
        in_specs=(P("tok", "col"), P("col", "tok"), P("col"), P(None, "tok")),
        out_specs=(P("col", "tok"), P("col", None)),
        check_vma=False,
    )
```

```python
import jax
import jax.numpy as jnp
from jax import lax
from jax.experimental import pallas as pl
from jax.experimental.pallas import tpu as pltpu
from jax.sharding import PartitionSpec as P

MESH = pl.DeviceIdType.MESH
SLAB_DEV = 64
LANES = 128
CW = 1024
BLK = 512
NJ = 7
ORDER = (0, 4, 6, 1, 5, 2, 3)
SLAB_J = 2
CROSS_I, SHARE_I, PASS_I = 2, 4, 6
READY = ((2, 2, 3, 3, 5, 5, 5, 6), (6, 6, 2, 2, 4, 4, 4, 2))
X1, YP, YM, Y2, YPX, YMX, X2, OWN = range(8)


def kernel(
    x_hbm, codes_hbm, gi_hbm, scales_hbm, out_ref, hes_ref,
    xbuf, wbuf, codes, gi, scales, hi, mid, lo, oh, pbuf, rbuf, slab, st, hs, h1, acc,
    lsem, csem, line_s, line_r, sib_s, sib_r, slab_s, slab_r, d_s, d_r, e_s, e_r, es_s, es_r,
    h1_s, h1_r, h2_s, h2_r, crossing, d2_s, d2_r,
):
    c = lax.axis_index("col")
    t = lax.axis_index("tok")
    y, x, q = t // 4, (t // 2) % 2, t % 2
    p = t // 2
    rows, width = x_hbm.shape
    half = width // 2
    dcols = out_ref.shape[1] // 16
    groups = scales.shape[0]

    def slot(dy, dx):
        return ((y + dy) % 4) * 4 + ((x + dx) % 2) * 2 + q

    def sibling(s):
        return s + 1 - 2 * (s % 2)

    yp, ym, xn, sib = slot(1, 0), slot(3, 0), slot(0, 1), sibling(t)

    own = pltpu.make_async_copy(x_hbm, xbuf.at[t, :, pl.ds(0, width)], lsem.at[0])
    own.start()
    own_slab = pltpu.make_async_copy(x_hbm.at[:, pl.ds(0, LANES)], slab.at[c], lsem.at[3])
    own_slab.start()
    gi_cp = pltpu.make_async_copy(gi_hbm, gi, lsem.at[1])
    gi_cp.start()
    sc_cp = pltpu.make_async_copy(scales_hbm, scales, lsem.at[2])
    sc_cp.start()

    def code_copy(b):
        r = pl.ds(pl.multiple_of(b * BLK, BLK), BLK)
        return pltpu.make_async_copy(codes_hbm.at[r], codes.at[r], csem.at[b])

    @pl.loop(0, csem.shape[0])
    def _(b):
        code_copy(b).start()

    bar = pltpu.get_barrier_semaphore()

    def greet(cc, tt):
        pl.semaphore_signal(bar, inc=1, device_id=(cc, tt), device_id_type=MESH)

    for dy in range(4):
        for dx in range(2):
            if dy or dx:
                greet(c, slot(dy, dx))
    greet(c, sib)

    @pl.loop(1, 8)
    def _(d):
        greet((c + d) % 8, t)

    pl.semaphore_wait(bar, 15)

    def slab_copy(d):
        return pltpu.make_async_remote_copy(
            src_ref=x_hbm.at[:, pl.ds(0, LANES)], dst_ref=slab.at[c],
            send_sem=slab_s.at[d], recv_sem=slab_r.at[d],
            device_id=((c + d) % 8, t), device_id_type=MESH,
        )

    @pl.loop(1, 8)
    def _(d):
        slab_copy(d).start()

    def pick(i, values):
        out = values[0]
        for n in range(1, len(values)):
            out = jnp.where(i == n, values[n], out)
        return out

    def col0(j):
        return pl.multiple_of(pick(j, ORDER) * CW, CW)

    def line(kind, j, s, dev):
        cols = pl.ds(col0(j), CW)
        return pltpu.make_async_remote_copy(
            src_ref=xbuf.at[s, :, cols], dst_ref=xbuf.at[s, :, cols],
            send_sem=line_s.at[kind, j], recv_sem=line_r.at[kind, j],
            device_id=(c, dev), device_id_type=MESH,
        )

    def across(kind, j, s):
        cols = pl.ds(col0(j), CW)
        return pltpu.make_async_remote_copy(
            src_ref=xbuf.at[s, :, cols], dst_ref=xbuf.at[s, :, cols],
            send_sem=sib_s.at[kind, j], recv_sem=sib_r.at[kind, j],
            device_id=(c, sib), device_id_type=MESH,
        )

    slots = {
        X1: slot(0, 1), YP: slot(3, 0), YM: slot(1, 0), Y2: slot(2, 0),
        YPX: slot(3, 1), YMX: slot(1, 1), X2: slot(2, 1), OWN: t,
    }

    def got(kind, j):
        line(kind, j, slots[kind], yp).wait_recv()

    def got_sib(kind, j):
        across(kind, j, sibling(slots[kind])).wait_recv()

    def send_own(j):
        line(YP, j, t, yp).start()
        line(YM, j, t, ym).start()
        line(X1, j, t, xn).start()
        across(OWN, j, t).start()

    own.wait()
    for j in range(SLAB_J):
        send_own(j)

    sc_cp.wait()
    gi_cp.wait()
    for ref in (hi, mid, lo):
        ref[pl.ds(groups, 512 - groups), :] = jnp.zeros((512 - groups, dcols), jnp.bfloat16)

    @pl.loop(0, groups // 32)
    def _(i):
        r = pl.ds(pl.multiple_of(i * 32, 32), 32)
        s = scales[r, :]
        a = s.astype(jnp.bfloat16)
        rest = s - a.astype(jnp.float32)
        b = rest.astype(jnp.bfloat16)
        hi[r, :] = a
        mid[r, :] = b
        lo[r, :] = (rest - b.astype(jnp.float32)).astype(jnp.bfloat16)

    def dequant(b):
        code_copy(b).wait()
        ids = lax.broadcasted_iota(jnp.int32, (LANES, 512), 1).astype(jnp.float32)
        for r in range(BLK // LANES):
            g = gi[pl.ds(b * (BLK // LANES) + r, 1), :].astype(jnp.float32)
            g = jnp.transpose(jnp.broadcast_to(g, (LANES, LANES)))
            g = jnp.concatenate([g] * 4, axis=1)
            oh[pl.ds(r * LANES, LANES), :] = jnp.where(g == ids, 1.0, 0.0).astype(jnp.bfloat16)
        one = oh[...]
        s = (
            jnp.dot(one, hi[...], preferred_element_type=jnp.float32)
            + jnp.dot(one, mid[...], preferred_element_type=jnp.float32)
            + jnp.dot(one, lo[...], preferred_element_type=jnp.float32)
        )
        r = pl.ds(pl.multiple_of(b * BLK, BLK), BLK)
        wbuf[r, :] = (s * (codes[r, :].astype(jnp.float32) - 8.0)).astype(jnp.bfloat16)

    def slab_chunk():
        own_slab.wait()

        @pl.loop(1, 8)
        def _(d):
            slab_copy(d).wait_recv()

        for i in range(4):
            pair = jnp.concatenate([slab[2 * i][:, :SLAB_DEV], slab[2 * i + 1][:, :SLAB_DEV]], axis=1)
            xbuf[t, :, pl.ds(width + i * LANES, LANES)] = pair

    slab_chunk()

    @pl.loop(SLAB_J, NJ)
    def _(j):
        send_own(j)

    def arrive(kind, j):
        got(kind, j)
        across(kind, j, slots[kind]).start()

    @pl.loop(0, NJ)
    def _(j):
        dequant(2 * j)

        @pl.when(j < NJ - 1)
        def _():
            dequant(2 * j + 1)

        arrive(YP, j)
        arrive(YM, j)

        @pl.when(j % 2 == 0)
        def _():
            line(Y2, j, slots[YP], yp).start()

        @pl.when(j % 2 == 1)
        def _():
            line(Y2, j, slots[YM], ym).start()

        arrive(X1, j)

    @pl.loop(0, NJ)
    def _(j):
        line(YPX, j, slots[X1], yp).start()
        line(YMX, j, slots[X1], ym).start()

    def chunk_product(kinds, base, j):
        def part(n):
            r = pl.ds(col0(j), n)
            a = jnp.concatenate(
                [xbuf[pl.ds(2 * (slots[k] // 2), 2), :, r].reshape(2 * rows, n) for k in kinds], axis=0
            )
            prod = jnp.dot(a, wbuf[r, :], preferred_element_type=jnp.float32)
            acc[pl.ds(base, len(kinds))] += prod.reshape(len(kinds), 2 * rows, dcols)

        @pl.when(j != SLAB_J)
        def _():
            part(CW)

        @pl.when(j == SLAB_J)
        def _():
            part(CW // 2)

    xh, z = c // 4, c % 4

    def d_copy(k, same_x):
        if same_x:
            place, dev = 4 * (k // 4) + z, 4 * xh + k % 4
        else:
            place, dev = c, k
        return pltpu.make_async_remote_copy(
            src_ref=pbuf.at[k], dst_ref=rbuf.at[place],
            send_sem=d_s.at[k], recv_sem=d_r.at[place],
            device_id=(dev, t), device_id_type=MESH,
        )

    def stays(k, same_x):
        return k % 4 == z if same_x else k == c

    def send_terms(kinds, base):
        for i, kind in enumerate(kinds):
            k = slots[kind] // 2
            same_x = kind in (OWN, YP, YM, Y2)
            here = stays(k, same_x)

            @pl.when(here)
            def _():
                rbuf[4 * (k // 4) + z if same_x else c] = acc[base + i].astype(jnp.bfloat16)

            @pl.when(jnp.logical_not(here))
            def _():
                pbuf[k] = acc[base + i].astype(jnp.bfloat16)
                d_copy(k, same_x).start()

    def z_sum(kh):
        @pl.loop(1, 4)
        def _(d):
            s = 4 * kh + (z + d) % 4
            pltpu.make_async_remote_copy(
                src_ref=pbuf.at[s], dst_ref=rbuf.at[s], send_sem=d_s.at[s], recv_sem=d_r.at[s],
                device_id=(4 * xh + (z + d) % 4, t), device_id_type=MESH,
            ).wait_recv()

        total = rbuf[4 * kh].astype(jnp.float32)
        for i in range(1, 4):
            total += rbuf[4 * kh + i].astype(jnp.float32)
        return total

    cross_copy = pltpu.make_async_remote_copy(
        src_ref=crossing.at[0], dst_ref=crossing.at[1], send_sem=d2_s, recv_sem=d2_r,
        device_id=(4 * (1 - xh) + z, t), device_id_type=MESH,
    )

    def cross():
        crossing[0] = z_sum(1 - xh).astype(jnp.bfloat16)
        cross_copy.start()

    near = (OWN, X1, YP, YM)
    acc[...] = jnp.zeros_like(acc)

    @pl.loop(0, NJ)
    def _(j):
        arrive(Y2, j)
        line(X2, j, slots[Y2], xn).start()
        for kind in near:
            got_sib(kind, j)
        chunk_product(near, 0, j)

    send_terms(near, 0)

    @pl.loop(0, NJ)
    def _(j):
        got_sib(Y2, j)
        chunk_product((Y2,), 4, j)

    send_terms((Y2,), 4)

    def out_cols(s):
        return pl.ds(pl.multiple_of(s * dcols, dcols), dcols)

    def e_copy(s, d, dev):
        return pltpu.make_async_remote_copy(
            src_ref=out_ref.at[:, out_cols(s)], dst_ref=out_ref.at[:, out_cols(s)],
            send_sem=e_s.at[d], recv_sem=e_r.at[d],
            device_id=(c, dev), device_id_type=MESH,
        )

    def es_copy(s, d):
        return pltpu.make_async_remote_copy(
            src_ref=out_ref.at[:, out_cols(s)], dst_ref=out_ref.at[:, out_cols(s)],
            send_sem=es_s.at[d], recv_sem=es_r.at[d],
            device_id=(c, sib), device_id_type=MESH,
        )

    def share_total(total):
        out_ref[:, out_cols(t)] = total.astype(jnp.bfloat16)
        e_copy(t, 4, xn).start()
        for dy in (2, 1, 3):
            e_copy(t, dy, slot(dy, 0)).start()
        es_copy(t, 0).start()

    def share():
        total = z_sum(xh)
        cross_copy.wait_recv()
        share_total(total + crossing[1].astype(jnp.float32))

    def share_straight():
        @pl.loop(1, 8)
        def _(d):
            s = (c + d) % 8
            pltpu.make_async_remote_copy(
                src_ref=pbuf.at[s], dst_ref=rbuf.at[s], send_sem=d_s.at[s], recv_sem=d_r.at[s],
                device_id=(s, t), device_id_type=MESH,
            ).wait_recv()

        total = rbuf[0].astype(jnp.float32)
        for i in range(1, 8):
            total += rbuf[i].astype(jnp.float32)
        share_total(total)

    def pass_on():
        e_copy(xn, 4, xn).wait_recv()
        for dy in (2, 1, 3):
            e_copy(xn, 4 + dy, slot(dy, 0)).start()
        es_copy(xn, 4).start()

    wide = p % 4 == 0
    first = 3 * p + (p + 7) // 8 + (p + 3) // 8
    ready = jnp.where(q == 0, pick(p, READY[0]), pick(p, READY[1]))

    def h_part(i):
        src = pl.ds(pl.multiple_of(q * half + (first + i) * LANES, LANES), LANES)
        a = xbuf[:, :, src].reshape(16 * rows, LANES)
        r = jnp.dot(st[...], a, preferred_element_type=jnp.float32)
        dst = pl.ds(pl.multiple_of(i * LANES, LANES), LANES)
        hs[:, :, dst] = r.astype(jnp.bfloat16).reshape(8, SLAB_DEV, LANES)

    def h1_copy(k, n):
        cols = pl.ds(0, n * LANES)
        return pltpu.make_async_remote_copy(
            src_ref=hs.at[k, :, cols], dst_ref=h1.at[c, :, cols],
            send_sem=h1_s.at[k], recv_sem=h1_r.at[c],
            device_id=(k, t), device_id_type=MESH,
        )

    def h1_wait(s, n):
        cols = pl.ds(0, n * LANES)
        pltpu.make_async_remote_copy(
            src_ref=hs.at[s, :, cols], dst_ref=h1.at[s, :, cols],
            send_sem=h1_s.at[s], recv_sem=h1_r.at[s],
            device_id=(s, t), device_id_type=MESH,
        ).wait_recv()

    def either(f):
        @pl.when(wide)
        def _():
            f(4)

        @pl.when(jnp.logical_not(wide))
        def _():
            f(3)

    def hessian():
        @pl.loop(0, 4)
        def _(i):
            @pl.when(jnp.logical_or(i < 3, wide))
            def _():
                h_part(i)

        h1[c] = hs[c]

        @pl.loop(1, 8)
        def _(d):
            either(lambda n: h1_copy((c + d) % 8, n).start())

    far = (YPX, YMX)
    early = c % 2 == x
    even = (c // 2 - y) % 2 == 0

    @pl.loop(0, NJ + 1)
    def _(i):
        @pl.when(i == 0)
        def _():
            arrive(X2, 0)
            arrive(X2, 1)

        @pl.when(i < NJ - 2)
        def _():
            arrive(X2, i + 2)

        @pl.when(jnp.logical_and(i >= 1, i < NJ - 1))
        def _():
            @pl.when(i == 1)
            def _():
                for j in range(2):
                    got_sib(X2, j)
                    chunk_product((X2,), 5, j)

            got_sib(X2, i + 1)
            chunk_product((X2,), 5, i + 1)

        @pl.when(i == NJ - 2)
        def _():
            send_terms((X2,), 5)

        @pl.when(jnp.logical_and(early, i == CROSS_I))
        def _():
            cross()

        @pl.when(jnp.logical_and(early, i == SHARE_I))
        def _():
            share()

        @pl.when(jnp.logical_and(jnp.logical_not(early), i == PASS_I))
        def _():
            pass_on()

        @pl.when(i < NJ)
        def _():
            arrive(YPX, i)
            arrive(YMX, i)

        @pl.when(i > 0)
        def _():
            for kind in far:
                got_sib(kind, i - 1)
            chunk_product(far, 6, i - 1)

        @pl.when(i == SLAB_J + 1)
        def _():
            @pl.loop(0, 4)
            def _(k):
                src = pl.ds(pl.multiple_of(width + k * LANES, LANES), LANES)
                a = xbuf[:, :, src].reshape(16 * rows, LANES).astype(jnp.float32)
                st[pl.ds(pl.multiple_of(k * LANES, LANES), LANES), :] = jnp.transpose(a).astype(jnp.bfloat16)

        @pl.when(i == NJ)
        def _():
            send_terms(far, 6)

        @pl.when(i - 1 == ready)
        def _():
            hessian()

    @pl.when(jnp.logical_and(jnp.logical_not(early), even))
    def _():
        share_straight()

    @pl.when(jnp.logical_and(early, even))
    def _():
        pass_on()

    @pl.when(jnp.logical_and(jnp.logical_not(early), jnp.logical_not(even)))
    def _():
        share_straight()

    def place(s):
        return 2 * s + q

    def h2_copy(s, n):
        dst = hes_ref.at[:, pl.ds(pl.multiple_of(first * LANES, LANES), n * LANES)]
        return pltpu.make_async_remote_copy(
            src_ref=h1.at[s, :, pl.ds(0, n * LANES)], dst_ref=dst,
            send_sem=h2_s.at[s], recv_sem=h2_r.at[p],
            device_id=(c, place(s)), device_id_type=MESH,
        )

    def h2_wait(s, n):
        f = 3 * s + (s + 7) // 8 + (s + 3) // 8
        dst = hes_ref.at[:, pl.ds(pl.multiple_of(f * LANES, LANES), n * LANES)]
        pltpu.make_async_remote_copy(
            src_ref=h1.at[s, :, pl.ds(0, n * LANES)], dst_ref=dst,
            send_sem=h2_s.at[s], recv_sem=h2_r.at[s],
            device_id=(c, place(s)), device_id_type=MESH,
        ).wait_recv()

    @pl.loop(1, 8)
    def _(d):
        either(lambda n: h1_wait((c + d) % 8, n))

    @pl.loop(1, 8)
    def _(d):
        either(lambda n: h2_copy((p + d) % 8, n).start())

    def keep(n):
        hes_ref[:, pl.ds(pl.multiple_of(first * LANES, LANES), n * LANES)] = h1[p, :, pl.ds(0, n * LANES)]

    either(keep)

    def own_line():
        for dy in (1, 3, 2):
            s = slot(-dy % 4, 0)
            e_copy(s, dy, xn).wait_recv()
            es_copy(s, dy).start()

    def other_line():
        for dy in (1, 3, 2):
            s = slot(-dy % 4, 1)
            e_copy(s, 4 + dy, xn).wait_recv()
            es_copy(s, 4 + dy).start()

    @pl.when(early)
    def _():
        own_line()

        @pl.when(jnp.logical_not(even))
        def _():
            pass_on()

        other_line()

    @pl.when(jnp.logical_not(early))
    def _():
        other_line()
        own_line()

    for d in range(8):
        s = slot(-(d % 4) % 4, d // 4)
        es_copy(sibling(s), d).wait_recv()

    for s in range(8):
        @pl.when(s != p)
        def _():
            h2_wait(s, 4 if s % 4 == 0 else 3)

    @pl.loop(1, 8)
    def _(d):
        either(lambda n: h1_copy((c + d) % 8, n).wait_send())
        either(lambda n: h2_copy((p + d) % 8, n).wait_send())
        slab_copy(d).wait_send()

    @pl.loop(0, 8)
    def _(k):
        @pl.when(jnp.where(k % 2 == x, k % 4 != z, k != c))
        def _():
            d_copy(k, True).wait_send()

    @pl.when(early)
    def _():
        cross_copy.wait_send()

    for d in range(8):
        es_copy(t, d).wait_send()
        if d:
            e_copy(t, d, sib).wait_send()

    @pl.loop(0, NJ)
    def _(j):
        for kind in range(8):
            if kind != OWN:
                line(kind, j, t, yp).wait_send()
            across(kind, j, t).wait_send()


def fused(tokens_in, codes, group_index, scales):
    rows, width = tokens_in.shape
    dcols = codes.shape[1]
    bf, f32 = jnp.bfloat16, jnp.float32
    dma = pltpu.SemaphoreType.DMA
    table = pltpu.VMEM((512, dcols), bf)
    return pl.pallas_call(
        kernel,
        name="calibrate",
        out_shape=(
            jax.ShapeDtypeStruct((128, 16 * dcols), bf),
            jax.ShapeDtypeStruct((SLAB_DEV, width // 2), bf),
        ),
        in_specs=[pl.BlockSpec(memory_space=pltpu.HBM)] * 4,
        out_specs=[pl.BlockSpec(memory_space=pltpu.VMEM)] * 2,
        scratch_shapes=[
            pltpu.VMEM((16, rows, NJ * CW), bf),
            pltpu.VMEM((width, dcols), bf),
            pltpu.VMEM((width, dcols), jnp.int32),
            pltpu.VMEM((width // LANES, LANES), jnp.int32),
            pltpu.VMEM(scales.shape, f32),
            table, table, table,
            pltpu.VMEM((BLK, 512), bf),
            pltpu.VMEM((8, 2 * rows, dcols), bf),
            pltpu.VMEM((8, 2 * rows, dcols), bf),
            pltpu.VMEM((8, rows, LANES), bf),
            pltpu.VMEM((512, 16 * rows), bf),
            pltpu.VMEM((8, SLAB_DEV, 512), bf),
            pltpu.VMEM((8, SLAB_DEV, 512), bf),
            pltpu.VMEM((8, 2 * rows, dcols), f32),
            dma((4,)), dma((width // BLK,)),
            dma((8, NJ)), dma((8, NJ)), dma((8, NJ)), dma((8, NJ)),
            dma((8,)), dma((8,)), dma((8,)), dma((8,)),
            dma((8,)), dma((8,)), dma((8,)), dma((8,)),
            dma((8,)), dma((8,)), dma((8,)), dma((8,)),
            pltpu.VMEM((2, 2 * rows, dcols), bf), dma, dma,
        ],
        compiler_params=pltpu.CompilerParams(
            collective_id=0, has_side_effects=True, vmem_limit_bytes=46 << 20
        ),
        cost_estimate=pl.CostEstimate(
            flops=16 * 10**9, bytes_accessed=20 * 10**6, transcendentals=0
        ),
    )(tokens_in, codes, group_index.reshape(width // LANES, LANES), scales)


def local(tokens_in, codes, group_index, scales):
    total_tokens = tokens_in.shape[0] * lax.axis_size("tok")
    next_input, hessian = fused(tokens_in, codes, group_index, scales)
    return hessian.astype(jnp.float32) * (2.0 / total_tokens), next_input


def solution(mesh):
    return jax.shard_map(
        local,
        mesh=mesh,
        in_specs=(P("tok", "col"), P("col", "tok"), P("col"), P(None, "tok")),
        out_specs=(P("col", "tok"), P("col", None)),
        check_vma=False,
    )
```

```python
import jax
import jax.numpy as jnp
from jax import lax
from jax.experimental import pallas as pl
from jax.experimental.pallas import tpu as pltpu
from jax.sharding import PartitionSpec as P

MESH = pl.DeviceIdType.MESH
SLAB_DEV = 64
LANES = 128
CW = 1024
BLK = 512
NJ = 7
ORDER = (0, 4, 6, 1, 5, 2, 3)
SLAB_J = 2
CROSS_I, SHARE_I = 2, 4
READY = ((2, 2, 3, 3, 5, 5, 5, 6), (6, 6, 2, 2, 4, 4, 4, 2))
X1, YP, YM, Y2, YPX, YMX, X2, OWN = range(8)


def kernel(
    x_hbm, codes_hbm, gi_hbm, scales_hbm, out_ref, hes_ref,
    xbuf, wbuf, codes, gi, scales, hi, mid, lo, oh, pbuf, rbuf, slab, st, hs, h1, acc,
    lsem, csem, line_s, line_r, sib_s, sib_r, slab_s, slab_r, d_s, d_r, e_s, e_r, es_s, es_r,
    h1_s, h1_r, h2_s, h2_r, crossing, d2_s, d2_r,
):
    c = lax.axis_index("col")
    t = lax.axis_index("tok")
    y, x, q = t // 4, (t // 2) % 2, t % 2
    p = t // 2
    rows, width = x_hbm.shape
    half = width // 2
    dcols = out_ref.shape[1] // 16
    groups = scales.shape[0]

    def slot(dy, dx):
        return ((y + dy) % 4) * 4 + ((x + dx) % 2) * 2 + q

    def sibling(s):
        return s + 1 - 2 * (s % 2)

    yp, ym, xn, sib = slot(1, 0), slot(3, 0), slot(0, 1), sibling(t)

    own = pltpu.make_async_copy(x_hbm, xbuf.at[t, :, pl.ds(0, width)], lsem.at[0])
    own.start()
    own_slab = pltpu.make_async_copy(x_hbm.at[:, pl.ds(0, LANES)], slab.at[c], lsem.at[3])
    own_slab.start()
    gi_cp = pltpu.make_async_copy(gi_hbm, gi, lsem.at[1])
    gi_cp.start()
    sc_cp = pltpu.make_async_copy(scales_hbm, scales, lsem.at[2])
    sc_cp.start()

    def code_copy(b):
        r = pl.ds(pl.multiple_of(b * BLK, BLK), BLK)
        return pltpu.make_async_copy(codes_hbm.at[r], codes.at[r], csem.at[b])

    @pl.loop(0, csem.shape[0])
    def _(b):
        code_copy(b).start()

    bar = pltpu.get_barrier_semaphore()

    def greet(cc, tt):
        pl.semaphore_signal(bar, inc=1, device_id=(cc, tt), device_id_type=MESH)

    for dy in range(4):
        for dx in range(2):
            if dy or dx:
                greet(c, slot(dy, dx))
    greet(c, sib)

    @pl.loop(1, 8)
    def _(d):
        greet((c + d) % 8, t)

    pl.semaphore_wait(bar, 15)

    def slab_copy(d):
        return pltpu.make_async_remote_copy(
            src_ref=x_hbm.at[:, pl.ds(0, LANES)], dst_ref=slab.at[c],
            send_sem=slab_s.at[d], recv_sem=slab_r.at[d],
            device_id=((c + d) % 8, t), device_id_type=MESH,
        )

    @pl.loop(1, 8)
    def _(d):
        slab_copy(d).start()

    def pick(i, values):
        out = values[0]
        for n in range(1, len(values)):
            out = jnp.where(i == n, values[n], out)
        return out

    def col0(j):
        return pl.multiple_of(pick(j, ORDER) * CW, CW)

    def line(kind, j, s, dev):
        cols = pl.ds(col0(j), CW)
        return pltpu.make_async_remote_copy(
            src_ref=xbuf.at[s, :, cols], dst_ref=xbuf.at[s, :, cols],
            send_sem=line_s.at[kind, j], recv_sem=line_r.at[kind, j],
            device_id=(c, dev), device_id_type=MESH,
        )

    def across(kind, j, s):
        cols = pl.ds(col0(j), CW)
        return pltpu.make_async_remote_copy(
            src_ref=xbuf.at[s, :, cols], dst_ref=xbuf.at[s, :, cols],
            send_sem=sib_s.at[kind, j], recv_sem=sib_r.at[kind, j],
            device_id=(c, sib), device_id_type=MESH,
        )

    slots = {
        X1: slot(0, 1), YP: slot(3, 0), YM: slot(1, 0), Y2: slot(2, 0),
        YPX: slot(3, 1), YMX: slot(1, 1), X2: slot(2, 1), OWN: t,
    }

    def got(kind, j):
        line(kind, j, slots[kind], yp).wait_recv()

    def got_sib(kind, j):
        across(kind, j, sibling(slots[kind])).wait_recv()

    def send_own(j):
        line(YP, j, t, yp).start()
        line(YM, j, t, ym).start()
        line(X1, j, t, xn).start()
        across(OWN, j, t).start()

    own.wait()
    for j in range(SLAB_J):
        send_own(j)

    sc_cp.wait()
    gi_cp.wait()
    for ref in (hi, mid, lo):
        ref[pl.ds(groups, 512 - groups), :] = jnp.zeros((512 - groups, dcols), jnp.bfloat16)

    @pl.loop(0, groups // 32)
    def _(i):
        r = pl.ds(pl.multiple_of(i * 32, 32), 32)
        s = scales[r, :]
        a = s.astype(jnp.bfloat16)
        rest = s - a.astype(jnp.float32)
        b = rest.astype(jnp.bfloat16)
        hi[r, :] = a
        mid[r, :] = b
        lo[r, :] = (rest - b.astype(jnp.float32)).astype(jnp.bfloat16)

    def dequant(b):
        code_copy(b).wait()
        ids = lax.broadcasted_iota(jnp.int32, (LANES, 512), 1).astype(jnp.float32)
        for r in range(BLK // LANES):
            g = gi[pl.ds(b * (BLK // LANES) + r, 1), :].astype(jnp.float32)
            g = jnp.transpose(jnp.broadcast_to(g, (LANES, LANES)))
            g = jnp.concatenate([g] * 4, axis=1)
            oh[pl.ds(r * LANES, LANES), :] = jnp.where(g == ids, 1.0, 0.0).astype(jnp.bfloat16)
        one = oh[...]
        s = (
            jnp.dot(one, hi[...], preferred_element_type=jnp.float32)
            + jnp.dot(one, mid[...], preferred_element_type=jnp.float32)
            + jnp.dot(one, lo[...], preferred_element_type=jnp.float32)
        )
        r = pl.ds(pl.multiple_of(b * BLK, BLK), BLK)
        wbuf[r, :] = (s * (codes[r, :].astype(jnp.float32) - 8.0)).astype(jnp.bfloat16)

    def slab_chunk():
        own_slab.wait()

        @pl.loop(1, 8)
        def _(d):
            slab_copy(d).wait_recv()

        for i in range(4):
            pair = jnp.concatenate([slab[2 * i][:, :SLAB_DEV], slab[2 * i + 1][:, :SLAB_DEV]], axis=1)
            xbuf[t, :, pl.ds(width + i * LANES, LANES)] = pair

    slab_chunk()

    @pl.loop(SLAB_J, NJ)
    def _(j):
        send_own(j)

    def arrive(kind, j):
        got(kind, j)
        across(kind, j, slots[kind]).start()

    @pl.loop(0, NJ)
    def _(j):
        dequant(2 * j)

        @pl.when(j < NJ - 1)
        def _():
            dequant(2 * j + 1)

        arrive(YP, j)
        arrive(YM, j)

        @pl.when(j % 2 == 0)
        def _():
            line(Y2, j, slots[YP], yp).start()

        @pl.when(j % 2 == 1)
        def _():
            line(Y2, j, slots[YM], ym).start()

        arrive(X1, j)

    @pl.loop(0, NJ)
    def _(j):
        line(YPX, j, slots[X1], yp).start()
        line(YMX, j, slots[X1], ym).start()

    def chunk_product(kinds, base, j):
        def part(n):
            r = pl.ds(col0(j), n)
            a = jnp.concatenate(
                [xbuf[pl.ds(2 * (slots[k] // 2), 2), :, r].reshape(2 * rows, n) for k in kinds], axis=0
            )
            prod = jnp.dot(a, wbuf[r, :], preferred_element_type=jnp.float32)
            acc[pl.ds(base, len(kinds))] += prod.reshape(len(kinds), 2 * rows, dcols)

        @pl.when(j != SLAB_J)
        def _():
            part(CW)

        @pl.when(j == SLAB_J)
        def _():
            part(CW // 2)

    xh, z = c // 4, c % 4

    def d_copy(k, same_x):
        if same_x:
            place, dev = 4 * (k // 4) + z, 4 * xh + k % 4
        else:
            place, dev = c, k
        return pltpu.make_async_remote_copy(
            src_ref=pbuf.at[k], dst_ref=rbuf.at[place],
            send_sem=d_s.at[k], recv_sem=d_r.at[place],
            device_id=(dev, t), device_id_type=MESH,
        )

    def stays(k, same_x):
        return k % 4 == z if same_x else k == c

    def send_terms(kinds, base):
        for i, kind in enumerate(kinds):
            k = slots[kind] // 2
            same_x = kind in (OWN, YP, YM, Y2)
            here = stays(k, same_x)

            @pl.when(here)
            def _():
                rbuf[4 * (k // 4) + z if same_x else c] = acc[base + i].astype(jnp.bfloat16)

            @pl.when(jnp.logical_not(here))
            def _():
                pbuf[k] = acc[base + i].astype(jnp.bfloat16)
                d_copy(k, same_x).start()

    def z_sum(kh):
        @pl.loop(1, 4)
        def _(d):
            s = 4 * kh + (z + d) % 4
            pltpu.make_async_remote_copy(
                src_ref=pbuf.at[s], dst_ref=rbuf.at[s], send_sem=d_s.at[s], recv_sem=d_r.at[s],
                device_id=(4 * xh + (z + d) % 4, t), device_id_type=MESH,
            ).wait_recv()

        total = rbuf[4 * kh].astype(jnp.float32)
        for i in range(1, 4):
            total += rbuf[4 * kh + i].astype(jnp.float32)
        return total

    cross_copy = pltpu.make_async_remote_copy(
        src_ref=crossing.at[0], dst_ref=crossing.at[1], send_sem=d2_s, recv_sem=d2_r,
        device_id=(4 * (1 - xh) + z, t), device_id_type=MESH,
    )

    def cross():
        crossing[0] = z_sum(1 - xh).astype(jnp.bfloat16)
        cross_copy.start()

    near = (OWN, X1, YP, YM)
    acc[...] = jnp.zeros_like(acc)

    @pl.loop(0, NJ)
    def _(j):
        arrive(Y2, j)
        line(X2, j, slots[Y2], xn).start()
        for kind in near:
            got_sib(kind, j)
        chunk_product(near, 0, j)

    send_terms(near, 0)

    @pl.loop(0, NJ)
    def _(j):
        got_sib(Y2, j)
        chunk_product((Y2,), 4, j)

    send_terms((Y2,), 4)

    def out_cols(s):
        return pl.ds(pl.multiple_of(s * dcols, dcols), dcols)

    def e_copy(s, d, dev):
        return pltpu.make_async_remote_copy(
            src_ref=out_ref.at[:, out_cols(s)], dst_ref=out_ref.at[:, out_cols(s)],
            send_sem=e_s.at[d], recv_sem=e_r.at[d],
            device_id=(c, dev), device_id_type=MESH,
        )

    def es_copy(s, d):
        return pltpu.make_async_remote_copy(
            src_ref=out_ref.at[:, out_cols(s)], dst_ref=out_ref.at[:, out_cols(s)],
            send_sem=es_s.at[d], recv_sem=es_r.at[d],
            device_id=(c, sib), device_id_type=MESH,
        )

    def share_total(total):
        out_ref[:, out_cols(t)] = total.astype(jnp.bfloat16)
        e_copy(t, 4, xn).start()
        for dy in (2, 1, 3):
            e_copy(t, dy, slot(dy, 0)).start()
        es_copy(t, 0).start()

    def share():
        total = z_sum(xh)
        cross_copy.wait_recv()
        share_total(total + crossing[1].astype(jnp.float32))

    def share_straight():
        @pl.loop(1, 8)
        def _(d):
            s = (c + d) % 8
            pltpu.make_async_remote_copy(
                src_ref=pbuf.at[s], dst_ref=rbuf.at[s], send_sem=d_s.at[s], recv_sem=d_r.at[s],
                device_id=(s, t), device_id_type=MESH,
            ).wait_recv()

        total = rbuf[0].astype(jnp.float32)
        for i in range(1, 8):
            total += rbuf[i].astype(jnp.float32)
        share_total(total)

    def pass_on():
        e_copy(xn, 4, xn).wait_recv()
        for dy in (2, 1, 3):
            e_copy(xn, 4 + dy, slot(dy, 0)).start()
        es_copy(xn, 4).start()

    wide = p % 4 == 0
    first = 3 * p + (p + 7) // 8 + (p + 3) // 8
    ready = jnp.where(q == 0, pick(p, READY[0]), pick(p, READY[1]))

    def h_part(i, n):
        src = pl.ds(pl.multiple_of(q * half + (first + i) * LANES, LANES), n * LANES)
        a = xbuf[:, :, src].reshape(16 * rows, n * LANES)
        r = jnp.dot(st[...], a, preferred_element_type=jnp.float32)
        hs[:, :, pl.ds(i * LANES, n * LANES)] = r.astype(jnp.bfloat16).reshape(8, SLAB_DEV, n * LANES)

    def h1_copy(k, n):
        cols = pl.ds(0, n * LANES)
        return pltpu.make_async_remote_copy(
            src_ref=hs.at[k, :, cols], dst_ref=h1.at[c, :, cols],
            send_sem=h1_s.at[k], recv_sem=h1_r.at[c],
            device_id=(k, t), device_id_type=MESH,
        )

    def h1_wait(s, n):
        cols = pl.ds(0, n * LANES)
        pltpu.make_async_remote_copy(
            src_ref=hs.at[s, :, cols], dst_ref=h1.at[s, :, cols],
            send_sem=h1_s.at[s], recv_sem=h1_r.at[s],
            device_id=(s, t), device_id_type=MESH,
        ).wait_recv()

    def either(f):
        @pl.when(wide)
        def _():
            f(4)

        @pl.when(jnp.logical_not(wide))
        def _():
            f(3)

    def hessian():
        h_part(0, 3)

        @pl.when(wide)
        def _():
            h_part(3, 1)

        h1[c] = hs[c]

        @pl.loop(1, 8)
        def _(d):
            either(lambda n: h1_copy((c + d) % 8, n).start())

    far = (YPX, YMX)
    early = c % 2 == x
    even = (c // 2 - y) % 2 == 0

    @pl.loop(0, NJ - 1)
    def _(i):
        @pl.when(i == 0)
        def _():
            arrive(X2, 0)
            arrive(X2, 1)

        @pl.when(i < NJ - 2)
        def _():
            arrive(X2, i + 2)

        @pl.when(jnp.logical_and(i >= 1, i < NJ - 1))
        def _():
            @pl.when(i == 1)
            def _():
                for j in range(2):
                    got_sib(X2, j)
                    chunk_product((X2,), 5, j)

            got_sib(X2, i + 1)
            chunk_product((X2,), 5, i + 1)

        @pl.when(i == NJ - 2)
        def _():
            send_terms((X2,), 5)

        @pl.when(jnp.logical_and(early, i == CROSS_I))
        def _():
            cross()

        @pl.when(jnp.logical_and(early, i == SHARE_I))
        def _():
            share()

        arrive(YMX, i)
        arrive(YPX, i)

        @pl.when(i > 0)
        def _():
            for kind in far:
                got_sib(kind, i - 1)
            chunk_product(far, 6, i - 1)

        @pl.when(i == SLAB_J + 1)
        def _():
            @pl.loop(0, 4)
            def _(k):
                src = pl.ds(pl.multiple_of(width + k * LANES, LANES), LANES)
                a = xbuf[:, :, src].reshape(16 * rows, LANES).astype(jnp.float32)
                st[pl.ds(pl.multiple_of(k * LANES, LANES), LANES), :] = jnp.transpose(a).astype(jnp.bfloat16)

        @pl.when(i - 1 == ready)
        def _():
            hessian()

    arrive(YMX, NJ - 1)
    for kind in far:
        got_sib(kind, NJ - 2)
    chunk_product(far, 6, NJ - 2)
    for base, kind in ((7, YMX), (6, YPX)):
        if kind == YPX:
            @pl.when(jnp.logical_not(early))
            def _():
                pass_on()

            arrive(YPX, NJ - 1)
        got_sib(kind, NJ - 1)
        chunk_product((kind,), base, NJ - 1)
        send_terms((kind,), base)

    @pl.when(ready >= NJ - 2)
    def _():
        hessian()

    @pl.when(jnp.logical_and(jnp.logical_not(early), even))
    def _():
        share_straight()

    @pl.when(jnp.logical_and(early, even))
    def _():
        pass_on()

    def place(s):
        return 2 * s + q

    def h2_copy(s, n):
        dst = hes_ref.at[:, pl.ds(pl.multiple_of(first * LANES, LANES), n * LANES)]
        return pltpu.make_async_remote_copy(
            src_ref=h1.at[s, :, pl.ds(0, n * LANES)], dst_ref=dst,
            send_sem=h2_s.at[s], recv_sem=h2_r.at[p],
            device_id=(c, place(s)), device_id_type=MESH,
        )

    def h2_wait(s, n):
        f = 3 * s + (s + 7) // 8 + (s + 3) // 8
        dst = hes_ref.at[:, pl.ds(pl.multiple_of(f * LANES, LANES), n * LANES)]
        pltpu.make_async_remote_copy(
            src_ref=h1.at[s, :, pl.ds(0, n * LANES)], dst_ref=dst,
            send_sem=h2_s.at[s], recv_sem=h2_r.at[s],
            device_id=(c, place(s)), device_id_type=MESH,
        ).wait_recv()

    @pl.loop(1, 8)
    def _(d):
        either(lambda n: h1_wait((c + d) % 8, n))

    @pl.loop(1, 8)
    def _(d):
        either(lambda n: h2_copy((p + d) % 8, n).start())

    def keep(n):
        hes_ref[:, pl.ds(pl.multiple_of(first * LANES, LANES), n * LANES)] = h1[p, :, pl.ds(0, n * LANES)]

    either(keep)

    @pl.when(jnp.logical_and(jnp.logical_not(early), jnp.logical_not(even)))
    def _():
        share_straight()

    def own_line():
        for dy in (1, 3, 2):
            s = slot(-dy % 4, 0)
            e_copy(s, dy, xn).wait_recv()
            es_copy(s, dy).start()

    def other_line():
        for dy in (1, 3, 2):
            s = slot(-dy % 4, 1)
            e_copy(s, 4 + dy, xn).wait_recv()
            es_copy(s, 4 + dy).start()

    @pl.when(early)
    def _():
        own_line()

        @pl.when(jnp.logical_not(even))
        def _():
            pass_on()

        other_line()

    @pl.when(jnp.logical_not(early))
    def _():
        other_line()
        own_line()

    for d in range(8):
        s = slot(-(d % 4) % 4, d // 4)
        es_copy(sibling(s), d).wait_recv()

    for s in range(8):
        @pl.when(s != p)
        def _():
            h2_wait(s, 4 if s % 4 == 0 else 3)

    @pl.loop(1, 8)
    def _(d):
        either(lambda n: h1_copy((c + d) % 8, n).wait_send())
        either(lambda n: h2_copy((p + d) % 8, n).wait_send())
        slab_copy(d).wait_send()

    @pl.loop(0, 8)
    def _(k):
        @pl.when(jnp.where(k % 2 == x, k % 4 != z, k != c))
        def _():
            d_copy(k, True).wait_send()

    @pl.when(early)
    def _():
        cross_copy.wait_send()

    for d in range(8):
        es_copy(t, d).wait_send()
        if d:
            e_copy(t, d, sib).wait_send()

    @pl.loop(0, NJ)
    def _(j):
        for kind in range(8):
            if kind != OWN:
                line(kind, j, t, yp).wait_send()
            across(kind, j, t).wait_send()


def fused(tokens_in, codes, group_index, scales):
    rows, width = tokens_in.shape
    dcols = codes.shape[1]
    bf, f32 = jnp.bfloat16, jnp.float32
    dma = pltpu.SemaphoreType.DMA
    table = pltpu.VMEM((512, dcols), bf)
    inputs = (tokens_in, codes, group_index.reshape(width // LANES, LANES), scales)
    return pl.pallas_call(
        kernel,
        name="calibrate",
        out_shape=(
            jax.ShapeDtypeStruct((128, 16 * dcols), bf),
            jax.ShapeDtypeStruct((SLAB_DEV, width // 2), bf),
        ),
        in_specs=[pl.BlockSpec(memory_space=pltpu.HBM)] * 4,
        out_specs=[pl.BlockSpec(memory_space=pltpu.VMEM)] * 2,
        scratch_shapes=[
            pltpu.VMEM((16, rows, NJ * CW), bf),
            pltpu.VMEM((width, dcols), bf),
            pltpu.VMEM((width, dcols), jnp.int32),
            pltpu.VMEM((width // LANES, LANES), jnp.int32),
            pltpu.VMEM(scales.shape, f32),
            table, table, table,
            pltpu.VMEM((BLK, 512), bf),
            pltpu.VMEM((8, 2 * rows, dcols), bf),
            pltpu.VMEM((8, 2 * rows, dcols), bf),
            pltpu.VMEM((8, rows, LANES), bf),
            pltpu.VMEM((512, 16 * rows), bf),
            pltpu.VMEM((8, SLAB_DEV, 512), bf),
            pltpu.VMEM((8, SLAB_DEV, 512), bf),
            pltpu.VMEM((8, 2 * rows, dcols), f32),
            dma((4,)), dma((width // BLK,)),
            dma((8, NJ)), dma((8, NJ)), dma((8, NJ)), dma((8, NJ)),
            dma((8,)), dma((8,)), dma((8,)), dma((8,)),
            dma((8,)), dma((8,)), dma((8,)), dma((8,)),
            dma((8,)), dma((8,)), dma((8,)), dma((8,)),
            pltpu.VMEM((2, 2 * rows, dcols), bf), dma, dma,
        ],
        compiler_params=pltpu.CompilerParams(
            collective_id=0, has_side_effects=True, vmem_limit_bytes=46 << 20
        ),
        cost_estimate=pl.CostEstimate(
            flops=16 * 10**9, bytes_accessed=20 * 10**6, transcendentals=0
        ),
    )(*(pltpu.with_memory_space_constraint(v, pltpu.HBM) for v in inputs))


def local(tokens_in, codes, group_index, scales):
    total_tokens = tokens_in.shape[0] * lax.axis_size("tok")
    next_input, hessian = fused(tokens_in, codes, group_index, scales)
    return hessian.astype(jnp.float32) * (2.0 / total_tokens), next_input


def solution(mesh):
    return jax.shard_map(
        local,
        mesh=mesh,
        in_specs=(P("tok", "col"), P("col", "tok"), P("col"), P(None, "tok")),
        out_specs=(P("col", "tok"), P("col", None)),
        check_vma=False,
    )
```

```python
import jax
import jax.numpy as jnp
from jax import lax
from jax.experimental import pallas as pl
from jax.experimental.pallas import tpu as pltpu
from jax.sharding import PartitionSpec as P

MESH = pl.DeviceIdType.MESH
SLAB_DEV = 64
LANES = 128
CW = 1024
BLK = 512
NJ = 7
ORDER = (0, 4, 6, 1, 5, 2, 3)
SLAB_J = 2
CROSS_I, SHARE_I = 3, 5
READY = ((2, 2, 3, 3, 5, 5, 5, 6), (6, 6, 2, 2, 4, 4, 4, 2))
X1, YP, YM, Y2, YPX, YMX, X2, OWN = range(8)


def kernel(
    x_hbm, codes_hbm, gi_hbm, scales_hbm, out_ref, hes_ref,
    xbuf, wbuf, codes, gi, scales, hi, mid, lo, oh, pbuf, rbuf, slab, st, hs, h1, acc,
    lsem, csem, line_s, line_r, sib_s, sib_r, slab_s, slab_r, d_s, d_r, e_s, e_r, es_s, es_r,
    h1_s, h1_r, h2_s, h2_r, crossing, d2_s, d2_r,
):
    c = lax.axis_index("col")
    t = lax.axis_index("tok")
    y, x, q = t // 4, (t // 2) % 2, t % 2
    p = t // 2
    rows, width = x_hbm.shape
    half = width // 2
    dcols = out_ref.shape[1] // 16
    groups = scales.shape[0]

    def slot(dy, dx):
        return ((y + dy) % 4) * 4 + ((x + dx) % 2) * 2 + q

    def sibling(s):
        return s + 1 - 2 * (s % 2)

    yp, ym, xn, sib = slot(1, 0), slot(3, 0), slot(0, 1), sibling(t)

    own = pltpu.make_async_copy(x_hbm, xbuf.at[t, :, pl.ds(0, width)], lsem.at[0])
    own.start()
    own_slab = pltpu.make_async_copy(x_hbm.at[:, pl.ds(0, LANES)], slab.at[c], lsem.at[3])
    own_slab.start()
    gi_cp = pltpu.make_async_copy(gi_hbm, gi, lsem.at[1])
    gi_cp.start()
    sc_cp = pltpu.make_async_copy(scales_hbm, scales, lsem.at[2])
    sc_cp.start()

    def code_copy(b):
        r = pl.ds(pl.multiple_of(b * BLK, BLK), BLK)
        return pltpu.make_async_copy(codes_hbm.at[r], codes.at[r], csem.at[b])

    @pl.loop(0, csem.shape[0])
    def _(b):
        code_copy(b).start()

    bar = pltpu.get_barrier_semaphore()

    def greet(cc, tt):
        pl.semaphore_signal(bar, inc=1, device_id=(cc, tt), device_id_type=MESH)

    for dy in range(4):
        for dx in range(2):
            if dy or dx:
                greet(c, slot(dy, dx))
    greet(c, sib)

    @pl.loop(1, 8)
    def _(d):
        greet((c + d) % 8, t)

    pl.semaphore_wait(bar, 15)

    def slab_copy(d):
        return pltpu.make_async_remote_copy(
            src_ref=x_hbm.at[:, pl.ds(0, LANES)], dst_ref=slab.at[c],
            send_sem=slab_s.at[d], recv_sem=slab_r.at[d],
            device_id=((c + d) % 8, t), device_id_type=MESH,
        )

    @pl.loop(1, 8)
    def _(d):
        slab_copy(d).start()

    def pick(i, values):
        out = values[0]
        for n in range(1, len(values)):
            out = jnp.where(i == n, values[n], out)
        return out

    def col0(j):
        return pl.multiple_of(pick(j, ORDER) * CW, CW)

    def line(kind, j, s, dev):
        cols = pl.ds(col0(j), CW)
        return pltpu.make_async_remote_copy(
            src_ref=xbuf.at[s, :, cols], dst_ref=xbuf.at[s, :, cols],
            send_sem=line_s.at[kind, j], recv_sem=line_r.at[kind, j],
            device_id=(c, dev), device_id_type=MESH,
        )

    def across(kind, j, s):
        cols = pl.ds(col0(j), CW)
        return pltpu.make_async_remote_copy(
            src_ref=xbuf.at[s, :, cols], dst_ref=xbuf.at[s, :, cols],
            send_sem=sib_s.at[kind, j], recv_sem=sib_r.at[kind, j],
            device_id=(c, sib), device_id_type=MESH,
        )

    slots = {
        X1: slot(0, 1), YP: slot(3, 0), YM: slot(1, 0), Y2: slot(2, 0),
        YPX: slot(3, 1), YMX: slot(1, 1), X2: slot(2, 1), OWN: t,
    }

    def got(kind, j):
        line(kind, j, slots[kind], yp).wait_recv()

    def got_sib(kind, j):
        across(kind, j, sibling(slots[kind])).wait_recv()

    def send_own(j):
        line(YP, j, t, yp).start()
        line(YM, j, t, ym).start()
        line(X1, j, t, xn).start()
        across(OWN, j, t).start()

    own.wait()
    for j in range(SLAB_J):
        send_own(j)

    sc_cp.wait()
    gi_cp.wait()
    for ref in (hi, mid, lo):
        ref[pl.ds(groups, 512 - groups), :] = jnp.zeros((512 - groups, dcols), jnp.bfloat16)

    @pl.loop(0, groups // 32)
    def _(i):
        r = pl.ds(pl.multiple_of(i * 32, 32), 32)
        s = scales[r, :]
        a = s.astype(jnp.bfloat16)
        rest = s - a.astype(jnp.float32)
        b = rest.astype(jnp.bfloat16)
        hi[r, :] = a
        mid[r, :] = b
        lo[r, :] = (rest - b.astype(jnp.float32)).astype(jnp.bfloat16)

    def dequant(b):
        code_copy(b).wait()
        ids = lax.broadcasted_iota(jnp.int32, (LANES, 512), 1).astype(jnp.float32)
        for r in range(BLK // LANES):
            g = gi[pl.ds(b * (BLK // LANES) + r, 1), :].astype(jnp.float32)
            g = jnp.transpose(jnp.broadcast_to(g, (LANES, LANES)))
            g = jnp.concatenate([g] * 4, axis=1)
            oh[pl.ds(r * LANES, LANES), :] = jnp.where(g == ids, 1.0, 0.0).astype(jnp.bfloat16)
        one = oh[...]
        s = (
            jnp.dot(one, hi[...], preferred_element_type=jnp.float32)
            + jnp.dot(one, mid[...], preferred_element_type=jnp.float32)
            + jnp.dot(one, lo[...], preferred_element_type=jnp.float32)
        )
        r = pl.ds(pl.multiple_of(b * BLK, BLK), BLK)
        wbuf[r, :] = (s * (codes[r, :].astype(jnp.float32) - 8.0)).astype(jnp.bfloat16)

    def slab_chunk():
        own_slab.wait()

        @pl.loop(1, 8)
        def _(d):
            slab_copy(d).wait_recv()

        for i in range(4):
            pair = jnp.concatenate([slab[2 * i][:, :SLAB_DEV], slab[2 * i + 1][:, :SLAB_DEV]], axis=1)
            xbuf[t, :, pl.ds(width + i * LANES, LANES)] = pair

    slab_chunk()

    @pl.loop(SLAB_J, NJ)
    def _(j):
        send_own(j)

    def arrive(kind, j):
        got(kind, j)
        across(kind, j, slots[kind]).start()

    @pl.loop(0, NJ)
    def _(j):
        dequant(2 * j)

        @pl.when(j < NJ - 1)
        def _():
            dequant(2 * j + 1)

        arrive(YP, j)
        arrive(YM, j)

        @pl.when(j % 2 == 0)
        def _():
            line(Y2, j, slots[YP], yp).start()

        @pl.when(j % 2 == 1)
        def _():
            line(Y2, j, slots[YM], ym).start()

        arrive(X1, j)

    @pl.loop(0, NJ)
    def _(j):
        line(YPX, j, slots[X1], yp).start()
        line(YMX, j, slots[X1], ym).start()

    def chunk_product(kinds, base, j):
        def part(n):
            r = pl.ds(col0(j), n)
            a = jnp.concatenate(
                [xbuf[pl.ds(2 * (slots[k] // 2), 2), :, r].reshape(2 * rows, n) for k in kinds], axis=0
            )
            prod = jnp.dot(a, wbuf[r, :], preferred_element_type=jnp.float32)
            acc[pl.ds(base, len(kinds))] += prod.reshape(len(kinds), 2 * rows, dcols)

        @pl.when(j != SLAB_J)
        def _():
            part(CW)

        @pl.when(j == SLAB_J)
        def _():
            part(CW // 2)

    xh, z = c // 4, c % 4

    def d_copy(k, same_x):
        if same_x:
            place, dev = 4 * (k // 4) + z, 4 * xh + k % 4
        else:
            place, dev = c, k
        return pltpu.make_async_remote_copy(
            src_ref=pbuf.at[k], dst_ref=rbuf.at[place],
            send_sem=d_s.at[k], recv_sem=d_r.at[place],
            device_id=(dev, t), device_id_type=MESH,
        )

    def stays(k, same_x):
        return k % 4 == z if same_x else k == c

    def send_terms(kinds, base):
        for i, kind in enumerate(kinds):
            k = slots[kind] // 2
            same_x = kind in (OWN, YP, YM, Y2)
            here = stays(k, same_x)

            @pl.when(here)
            def _():
                rbuf[4 * (k // 4) + z if same_x else c] = acc[base + i].astype(jnp.bfloat16)

            @pl.when(jnp.logical_not(here))
            def _():
                pbuf[k] = acc[base + i].astype(jnp.bfloat16)
                d_copy(k, same_x).start()

    def z_sum(kh):
        @pl.loop(1, 4)
        def _(d):
            s = 4 * kh + (z + d) % 4
            pltpu.make_async_remote_copy(
                src_ref=pbuf.at[s], dst_ref=rbuf.at[s], send_sem=d_s.at[s], recv_sem=d_r.at[s],
                device_id=(4 * xh + (z + d) % 4, t), device_id_type=MESH,
            ).wait_recv()

        total = rbuf[4 * kh].astype(jnp.float32)
        for i in range(1, 4):
            total += rbuf[4 * kh + i].astype(jnp.float32)
        return total

    cross_copy = pltpu.make_async_remote_copy(
        src_ref=crossing.at[0], dst_ref=crossing.at[1], send_sem=d2_s, recv_sem=d2_r,
        device_id=(4 * (1 - xh) + z, t), device_id_type=MESH,
    )

    def cross():
        crossing[0] = z_sum(1 - xh).astype(jnp.bfloat16)
        cross_copy.start()

    near = (OWN, X1, YP, YM)
    acc[...] = jnp.zeros_like(acc)

    @pl.loop(0, NJ)
    def _(j):
        arrive(Y2, j)
        line(X2, j, slots[Y2], xn).start()
        for kind in near:
            got_sib(kind, j)
        chunk_product(near, 0, j)

    send_terms(near, 0)

    @pl.loop(0, NJ)
    def _(j):
        got_sib(Y2, j)
        chunk_product((Y2,), 4, j)

    send_terms((Y2,), 4)

    def out_cols(s):
        return pl.ds(pl.multiple_of(s * dcols, dcols), dcols)

    def e_copy(s, d, dev):
        return pltpu.make_async_remote_copy(
            src_ref=out_ref.at[:, out_cols(s)], dst_ref=out_ref.at[:, out_cols(s)],
            send_sem=e_s.at[d], recv_sem=e_r.at[d],
            device_id=(c, dev), device_id_type=MESH,
        )

    def es_copy(s, d):
        return pltpu.make_async_remote_copy(
            src_ref=out_ref.at[:, out_cols(s)], dst_ref=out_ref.at[:, out_cols(s)],
            send_sem=es_s.at[d], recv_sem=es_r.at[d],
            device_id=(c, sib), device_id_type=MESH,
        )

    def share_total(total):
        out_ref[:, out_cols(t)] = total.astype(jnp.bfloat16)
        e_copy(t, 4, xn).start()
        for dy in (2, 1, 3):
            e_copy(t, dy, slot(dy, 0)).start()
        es_copy(t, 0).start()

    def share():
        total = z_sum(xh)
        cross_copy.wait_recv()
        share_total(total + crossing[1].astype(jnp.float32))

    def share_straight():
        @pl.loop(1, 8)
        def _(d):
            s = (c + d) % 8
            pltpu.make_async_remote_copy(
                src_ref=pbuf.at[s], dst_ref=rbuf.at[s], send_sem=d_s.at[s], recv_sem=d_r.at[s],
                device_id=(s, t), device_id_type=MESH,
            ).wait_recv()

        total = rbuf[0].astype(jnp.float32)
        for i in range(1, 8):
            total += rbuf[i].astype(jnp.float32)
        share_total(total)

    def pass_on():
        e_copy(xn, 4, xn).wait_recv()
        for dy in (2, 1, 3):
            e_copy(xn, 4 + dy, slot(dy, 0)).start()
        es_copy(xn, 4).start()

    wide = p % 4 == 0
    first = 3 * p + (p + 7) // 8 + (p + 3) // 8
    ready = jnp.where(q == 0, pick(p, READY[0]), pick(p, READY[1]))

    def h_part(i, n):
        src = pl.ds(pl.multiple_of(q * half + (first + i) * LANES, LANES), n * LANES)
        a = xbuf[:, :, src].reshape(16 * rows, n * LANES)
        r = jnp.dot(st[...], a, preferred_element_type=jnp.float32)
        hs[:, :, pl.ds(i * LANES, n * LANES)] = r.astype(jnp.bfloat16).reshape(8, SLAB_DEV, n * LANES)

    def h1_copy(k, n):
        cols = pl.ds(0, n * LANES)
        return pltpu.make_async_remote_copy(
            src_ref=hs.at[k, :, cols], dst_ref=h1.at[c, :, cols],
            send_sem=h1_s.at[k], recv_sem=h1_r.at[c],
            device_id=(k, t), device_id_type=MESH,
        )

    def h1_wait(s, n):
        cols = pl.ds(0, n * LANES)
        pltpu.make_async_remote_copy(
            src_ref=hs.at[s, :, cols], dst_ref=h1.at[s, :, cols],
            send_sem=h1_s.at[s], recv_sem=h1_r.at[s],
            device_id=(s, t), device_id_type=MESH,
        ).wait_recv()

    def either(f):
        @pl.when(wide)
        def _():
            f(4)

        @pl.when(jnp.logical_not(wide))
        def _():
            f(3)

    def hessian():
        h_part(0, 3)

        @pl.when(wide)
        def _():
            h_part(3, 1)

        h1[c] = hs[c]

        @pl.loop(1, 8)
        def _(d):
            either(lambda n: h1_copy((c + d) % 8, n).start())

    far = (YPX, YMX)
    early = c % 2 == x
    even = (c // 2 - y) % 2 == 0

    @pl.loop(0, NJ - 1)
    def _(i):
        @pl.when(i == 0)
        def _():
            arrive(X2, 0)
            arrive(X2, 1)

        @pl.when(i < NJ - 2)
        def _():
            arrive(X2, i + 2)

        @pl.when(jnp.logical_and(i >= 1, i < NJ - 1))
        def _():
            @pl.when(i == 1)
            def _():
                for j in range(2):
                    got_sib(X2, j)
                    chunk_product((X2,), 5, j)

            got_sib(X2, i + 1)
            chunk_product((X2,), 5, i + 1)

        @pl.when(i == NJ - 2)
        def _():
            send_terms((X2,), 5)

        @pl.when(jnp.logical_and(early, i == CROSS_I))
        def _():
            cross()

        @pl.when(jnp.logical_and(early, i == SHARE_I))
        def _():
            share()

        arrive(YMX, i)
        arrive(YPX, i)

        @pl.when(i > 0)
        def _():
            for kind in far:
                got_sib(kind, i - 1)
            chunk_product(far, 6, i - 1)

        @pl.when(i == SLAB_J + 1)
        def _():
            @pl.loop(0, 4)
            def _(k):
                src = pl.ds(pl.multiple_of(width + k * LANES, LANES), LANES)
                a = xbuf[:, :, src].reshape(16 * rows, LANES).astype(jnp.float32)
                st[pl.ds(pl.multiple_of(k * LANES, LANES), LANES), :] = jnp.transpose(a).astype(jnp.bfloat16)

        @pl.when(i - 1 == ready)
        def _():
            hessian()

    arrive(YMX, NJ - 1)
    for kind in far:
        got_sib(kind, NJ - 2)
    chunk_product(far, 6, NJ - 2)
    for base, kind in ((7, YMX), (6, YPX)):
        if kind == YPX:
            @pl.when(jnp.logical_not(early))
            def _():
                pass_on()

            arrive(YPX, NJ - 1)
        got_sib(kind, NJ - 1)
        chunk_product((kind,), base, NJ - 1)
        send_terms((kind,), base)

    @pl.when(ready >= NJ - 2)
    def _():
        hessian()

    @pl.when(jnp.logical_and(jnp.logical_not(early), even))
    def _():
        share_straight()

    @pl.when(jnp.logical_and(early, even))
    def _():
        pass_on()

    def place(s):
        return 2 * s + q

    def h2_copy(s, n):
        dst = hes_ref.at[:, pl.ds(pl.multiple_of(first * LANES, LANES), n * LANES)]
        return pltpu.make_async_remote_copy(
            src_ref=h1.at[s, :, pl.ds(0, n * LANES)], dst_ref=dst,
            send_sem=h2_s.at[s], recv_sem=h2_r.at[p],
            device_id=(c, place(s)), device_id_type=MESH,
        )

    def h2_wait(s, n):
        f = 3 * s + (s + 7) // 8 + (s + 3) // 8
        dst = hes_ref.at[:, pl.ds(pl.multiple_of(f * LANES, LANES), n * LANES)]
        pltpu.make_async_remote_copy(
            src_ref=h1.at[s, :, pl.ds(0, n * LANES)], dst_ref=dst,
            send_sem=h2_s.at[s], recv_sem=h2_r.at[s],
            device_id=(c, place(s)), device_id_type=MESH,
        ).wait_recv()

    @pl.loop(1, 8)
    def _(d):
        either(lambda n: h1_wait((c + d) % 8, n))

    @pl.loop(1, 8)
    def _(d):
        either(lambda n: h2_copy((p + d) % 8, n).start())

    def keep(n):
        hes_ref[:, pl.ds(pl.multiple_of(first * LANES, LANES), n * LANES)] = h1[p, :, pl.ds(0, n * LANES)]

    either(keep)

    @pl.when(jnp.logical_and(jnp.logical_not(early), jnp.logical_not(even)))
    def _():
        share_straight()

    def own_line():
        for dy in (1, 3, 2):
            s = slot(-dy % 4, 0)
            e_copy(s, dy, xn).wait_recv()
            es_copy(s, dy).start()

    def other_line():
        for dy in (1, 3, 2):
            s = slot(-dy % 4, 1)
            e_copy(s, 4 + dy, xn).wait_recv()
            es_copy(s, 4 + dy).start()

    @pl.when(early)
    def _():
        own_line()

        @pl.when(jnp.logical_not(even))
        def _():
            pass_on()

        other_line()

    @pl.when(jnp.logical_not(early))
    def _():
        other_line()
        own_line()

    for d in range(8):
        s = slot(-(d % 4) % 4, d // 4)
        es_copy(sibling(s), d).wait_recv()

    for s in range(8):
        @pl.when(s != p)
        def _():
            h2_wait(s, 4 if s % 4 == 0 else 3)

    @pl.loop(1, 8)
    def _(d):
        either(lambda n: h1_copy((c + d) % 8, n).wait_send())
        either(lambda n: h2_copy((p + d) % 8, n).wait_send())
        slab_copy(d).wait_send()

    @pl.loop(0, 8)
    def _(k):
        @pl.when(jnp.where(k % 2 == x, k % 4 != z, k != c))
        def _():
            d_copy(k, True).wait_send()

    @pl.when(early)
    def _():
        cross_copy.wait_send()

    for d in range(8):
        es_copy(t, d).wait_send()
        if d:
            e_copy(t, d, sib).wait_send()

    @pl.loop(0, NJ)
    def _(j):
        for kind in range(8):
            if kind != OWN:
                line(kind, j, t, yp).wait_send()
            across(kind, j, t).wait_send()


def fused(tokens_in, codes, group_index, scales):
    rows, width = tokens_in.shape
    dcols = codes.shape[1]
    bf, f32 = jnp.bfloat16, jnp.float32
    dma = pltpu.SemaphoreType.DMA
    table = pltpu.VMEM((512, dcols), bf)
    inputs = (tokens_in, codes, group_index.reshape(width // LANES, LANES), scales)
    return pl.pallas_call(
        kernel,
        name="calibrate",
        out_shape=(
            jax.ShapeDtypeStruct((128, 16 * dcols), bf),
            jax.ShapeDtypeStruct((SLAB_DEV, width // 2), bf),
        ),
        in_specs=[pl.BlockSpec(memory_space=pltpu.HBM)] * 4,
        out_specs=[pl.BlockSpec(memory_space=pltpu.VMEM)] * 2,
        scratch_shapes=[
            pltpu.VMEM((16, rows, NJ * CW), bf),
            pltpu.VMEM((width, dcols), bf),
            pltpu.VMEM((width, dcols), jnp.int32),
            pltpu.VMEM((width // LANES, LANES), jnp.int32),
            pltpu.VMEM(scales.shape, f32),
            table, table, table,
            pltpu.VMEM((BLK, 512), bf),
            pltpu.VMEM((8, 2 * rows, dcols), bf),
            pltpu.VMEM((8, 2 * rows, dcols), bf),
            pltpu.VMEM((8, rows, LANES), bf),
            pltpu.VMEM((512, 16 * rows), bf),
            pltpu.VMEM((8, SLAB_DEV, 512), bf),
            pltpu.VMEM((8, SLAB_DEV, 512), bf),
            pltpu.VMEM((8, 2 * rows, dcols), f32),
            dma((4,)), dma((width // BLK,)),
            dma((8, NJ)), dma((8, NJ)), dma((8, NJ)), dma((8, NJ)),
            dma((8,)), dma((8,)), dma((8,)), dma((8,)),
            dma((8,)), dma((8,)), dma((8,)), dma((8,)),
            dma((8,)), dma((8,)), dma((8,)), dma((8,)),
            pltpu.VMEM((2, 2 * rows, dcols), bf), dma, dma,
        ],
        compiler_params=pltpu.CompilerParams(
            collective_id=0, has_side_effects=True, vmem_limit_bytes=46 << 20
        ),
        cost_estimate=pl.CostEstimate(
            flops=16 * 10**9, bytes_accessed=20 * 10**6, transcendentals=0
        ),
    )(*(pltpu.with_memory_space_constraint(v, pltpu.HBM) for v in inputs))


def local(tokens_in, codes, group_index, scales):
    total_tokens = tokens_in.shape[0] * lax.axis_size("tok")
    next_input, hessian = fused(tokens_in, codes, group_index, scales)
    return hessian.astype(jnp.float32) * (2.0 / total_tokens), next_input


def solution(mesh):
    return jax.shard_map(
        local,
        mesh=mesh,
        in_specs=(P("tok", "col"), P("col", "tok"), P("col"), P(None, "tok")),
        out_specs=(P("col", "tok"), P("col", None)),
        check_vma=False,
    )
```

```python
import jax
import jax.numpy as jnp
from jax import lax
from jax.experimental import pallas as pl
from jax.experimental.pallas import tpu as pltpu
from jax.sharding import PartitionSpec as P

MESH = pl.DeviceIdType.MESH
SLAB_DEV = 64
LANES = 128
CW = 1024
BLK = 512
NJ = 7
ORDER = (0, 4, 6, 1, 5, 2, 3)
SLAB_J = 2
CROSS_I, SHARE_I = 2, 5
READY = ((2, 2, 3, 3, 5, 5, 5, 6), (6, 6, 2, 2, 4, 4, 4, 2))
X1, YP, YM, Y2, YPX, YMX, X2, OWN = range(8)


def kernel(
    x_hbm, codes_hbm, gi_hbm, scales_hbm, out_ref, hes_ref,
    xbuf, wbuf, codes, gi, scales, hi, mid, lo, oh, pbuf, rbuf, slab, st, hs, h1, acc,
    lsem, csem, line_s, line_r, sib_s, sib_r, slab_s, slab_r, d_s, d_r, e_s, e_r, es_s, es_r,
    h1_s, h1_r, h2_s, h2_r, crossing, d2_s, d2_r,
):
    c = lax.axis_index("col")
    t = lax.axis_index("tok")
    y, x, q = t // 4, (t // 2) % 2, t % 2
    p = t // 2
    rows, width = x_hbm.shape
    half = width // 2
    dcols = out_ref.shape[1] // 16
    groups = scales.shape[0]

    def slot(dy, dx):
        return ((y + dy) % 4) * 4 + ((x + dx) % 2) * 2 + q

    def sibling(s):
        return s + 1 - 2 * (s % 2)

    yp, ym, xn, sib = slot(1, 0), slot(3, 0), slot(0, 1), sibling(t)

    own = pltpu.make_async_copy(x_hbm, xbuf.at[t, :, pl.ds(0, width)], lsem.at[0])
    own.start()
    own_slab = pltpu.make_async_copy(x_hbm.at[:, pl.ds(0, LANES)], slab.at[c], lsem.at[3])
    own_slab.start()
    gi_cp = pltpu.make_async_copy(gi_hbm, gi, lsem.at[1])
    gi_cp.start()
    sc_cp = pltpu.make_async_copy(scales_hbm, scales, lsem.at[2])
    sc_cp.start()

    def code_copy(b):
        r = pl.ds(pl.multiple_of(b * BLK, BLK), BLK)
        return pltpu.make_async_copy(codes_hbm.at[r], codes.at[r], csem.at[b])

    @pl.loop(0, csem.shape[0])
    def _(b):
        code_copy(b).start()

    bar = pltpu.get_barrier_semaphore()

    def greet(cc, tt):
        pl.semaphore_signal(bar, inc=1, device_id=(cc, tt), device_id_type=MESH)

    for dy in range(4):
        for dx in range(2):
            if dy or dx:
                greet(c, slot(dy, dx))
    greet(c, sib)

    @pl.loop(1, 8)
    def _(d):
        greet((c + d) % 8, t)

    pl.semaphore_wait(bar, 15)

    def slab_copy(d):
        return pltpu.make_async_remote_copy(
            src_ref=x_hbm.at[:, pl.ds(0, LANES)], dst_ref=slab.at[c],
            send_sem=slab_s.at[d], recv_sem=slab_r.at[d],
            device_id=((c + d) % 8, t), device_id_type=MESH,
        )

    @pl.loop(1, 8)
    def _(d):
        slab_copy(d).start()

    def pick(i, values):
        out = values[0]
        for n in range(1, len(values)):
            out = jnp.where(i == n, values[n], out)
        return out

    def col0(j):
        return pl.multiple_of(pick(j, ORDER) * CW, CW)

    def line(kind, j, s, dev):
        cols = pl.ds(col0(j), CW)
        return pltpu.make_async_remote_copy(
            src_ref=xbuf.at[s, :, cols], dst_ref=xbuf.at[s, :, cols],
            send_sem=line_s.at[kind, j], recv_sem=line_r.at[kind, j],
            device_id=(c, dev), device_id_type=MESH,
        )

    def across(kind, j, s):
        cols = pl.ds(col0(j), CW)
        return pltpu.make_async_remote_copy(
            src_ref=xbuf.at[s, :, cols], dst_ref=xbuf.at[s, :, cols],
            send_sem=sib_s.at[kind, j], recv_sem=sib_r.at[kind, j],
            device_id=(c, sib), device_id_type=MESH,
        )

    slots = {
        X1: slot(0, 1), YP: slot(3, 0), YM: slot(1, 0), Y2: slot(2, 0),
        YPX: slot(3, 1), YMX: slot(1, 1), X2: slot(2, 1), OWN: t,
    }

    def got(kind, j):
        line(kind, j, slots[kind], yp).wait_recv()

    def got_sib(kind, j):
        across(kind, j, sibling(slots[kind])).wait_recv()

    def send_own(j):
        line(YP, j, t, yp).start()
        line(YM, j, t, ym).start()
        line(X1, j, t, xn).start()
        across(OWN, j, t).start()

    own.wait()
    for j in range(SLAB_J):
        send_own(j)

    sc_cp.wait()
    gi_cp.wait()
    for ref in (hi, mid, lo):
        ref[pl.ds(groups, 512 - groups), :] = jnp.zeros((512 - groups, dcols), jnp.bfloat16)

    @pl.loop(0, groups // 32)
    def _(i):
        r = pl.ds(pl.multiple_of(i * 32, 32), 32)
        s = scales[r, :]
        a = s.astype(jnp.bfloat16)
        rest = s - a.astype(jnp.float32)
        b = rest.astype(jnp.bfloat16)
        hi[r, :] = a
        mid[r, :] = b
        lo[r, :] = (rest - b.astype(jnp.float32)).astype(jnp.bfloat16)

    def dequant(b):
        code_copy(b).wait()
        ids = lax.broadcasted_iota(jnp.int32, (LANES, 512), 1).astype(jnp.float32)
        for r in range(BLK // LANES):
            g = gi[pl.ds(b * (BLK // LANES) + r, 1), :].astype(jnp.float32)
            g = jnp.transpose(jnp.broadcast_to(g, (LANES, LANES)))
            g = jnp.concatenate([g] * 4, axis=1)
            oh[pl.ds(r * LANES, LANES), :] = jnp.where(g == ids, 1.0, 0.0).astype(jnp.bfloat16)
        one = oh[...]
        s = (
            jnp.dot(one, hi[...], preferred_element_type=jnp.float32)
            + jnp.dot(one, mid[...], preferred_element_type=jnp.float32)
            + jnp.dot(one, lo[...], preferred_element_type=jnp.float32)
        )
        r = pl.ds(pl.multiple_of(b * BLK, BLK), BLK)
        wbuf[r, :] = (s * (codes[r, :].astype(jnp.float32) - 8.0)).astype(jnp.bfloat16)

    def slab_chunk():
        own_slab.wait()

        @pl.loop(1, 8)
        def _(d):
            slab_copy(d).wait_recv()

        for i in range(4):
            pair = jnp.concatenate([slab[2 * i][:, :SLAB_DEV], slab[2 * i + 1][:, :SLAB_DEV]], axis=1)
            xbuf[t, :, pl.ds(width + i * LANES, LANES)] = pair

    slab_chunk()

    @pl.loop(SLAB_J, NJ)
    def _(j):
        send_own(j)

    def arrive(kind, j):
        got(kind, j)
        across(kind, j, slots[kind]).start()

    @pl.loop(0, NJ)
    def _(j):
        dequant(2 * j)

        @pl.when(j < NJ - 1)
        def _():
            dequant(2 * j + 1)

        arrive(YP, j)
        arrive(YM, j)

        @pl.when(j % 2 == 0)
        def _():
            line(Y2, j, slots[YP], yp).start()

        @pl.when(j % 2 == 1)
        def _():
            line(Y2, j, slots[YM], ym).start()

        arrive(X1, j)

    @pl.loop(0, NJ)
    def _(j):
        line(YPX, j, slots[X1], yp).start()
        line(YMX, j, slots[X1], ym).start()

    def chunk_product(kinds, base, j):
        def part(n):
            r = pl.ds(col0(j), n)
            a = jnp.concatenate(
                [xbuf[pl.ds(2 * (slots[k] // 2), 2), :, r].reshape(2 * rows, n) for k in kinds], axis=0
            )
            prod = jnp.dot(a, wbuf[r, :], preferred_element_type=jnp.float32)
            acc[pl.ds(base, len(kinds))] += prod.reshape(len(kinds), 2 * rows, dcols)

        @pl.when(j != SLAB_J)
        def _():
            part(CW)

        @pl.when(j == SLAB_J)
        def _():
            part(CW // 2)

    xh, z = c // 4, c % 4

    def d_copy(k, same_x):
        if same_x:
            place, dev = 4 * (k // 4) + z, 4 * xh + k % 4
        else:
            place, dev = c, k
        return pltpu.make_async_remote_copy(
            src_ref=pbuf.at[k], dst_ref=rbuf.at[place],
            send_sem=d_s.at[k], recv_sem=d_r.at[place],
            device_id=(dev, t), device_id_type=MESH,
        )

    def stays(k, same_x):
        return k % 4 == z if same_x else k == c

    def send_terms(kinds, base):
        for i, kind in enumerate(kinds):
            k = slots[kind] // 2
            same_x = kind in (OWN, YP, YM, Y2)
            here = stays(k, same_x)

            @pl.when(here)
            def _():
                rbuf[4 * (k // 4) + z if same_x else c] = acc[base + i].astype(jnp.bfloat16)

            @pl.when(jnp.logical_not(here))
            def _():
                pbuf[k] = acc[base + i].astype(jnp.bfloat16)
                d_copy(k, same_x).start()

    def z_sum(kh):
        @pl.loop(1, 4)
        def _(d):
            s = 4 * kh + (z + d) % 4
            pltpu.make_async_remote_copy(
                src_ref=pbuf.at[s], dst_ref=rbuf.at[s], send_sem=d_s.at[s], recv_sem=d_r.at[s],
                device_id=(4 * xh + (z + d) % 4, t), device_id_type=MESH,
            ).wait_recv()

        total = rbuf[4 * kh].astype(jnp.float32)
        for i in range(1, 4):
            total += rbuf[4 * kh + i].astype(jnp.float32)
        return total

    cross_copy = pltpu.make_async_remote_copy(
        src_ref=crossing.at[0], dst_ref=crossing.at[1], send_sem=d2_s, recv_sem=d2_r,
        device_id=(4 * (1 - xh) + z, t), device_id_type=MESH,
    )

    def cross():
        crossing[0] = z_sum(1 - xh).astype(jnp.bfloat16)
        cross_copy.start()

    near = (OWN, X1, YP, YM)
    acc[...] = jnp.zeros_like(acc)

    @pl.loop(0, NJ)
    def _(j):
        arrive(Y2, j)
        line(X2, j, slots[Y2], xn).start()
        for kind in near:
            got_sib(kind, j)
        chunk_product(near, 0, j)

    send_terms(near, 0)

    @pl.loop(0, NJ)
    def _(j):
        got_sib(Y2, j)
        chunk_product((Y2,), 4, j)

    send_terms((Y2,), 4)

    def out_cols(s):
        return pl.ds(pl.multiple_of(s * dcols, dcols), dcols)

    def e_copy(s, d, dev):
        return pltpu.make_async_remote_copy(
            src_ref=out_ref.at[:, out_cols(s)], dst_ref=out_ref.at[:, out_cols(s)],
            send_sem=e_s.at[d], recv_sem=e_r.at[d],
            device_id=(c, dev), device_id_type=MESH,
        )

    def es_copy(s, d):
        return pltpu.make_async_remote_copy(
            src_ref=out_ref.at[:, out_cols(s)], dst_ref=out_ref.at[:, out_cols(s)],
            send_sem=es_s.at[d], recv_sem=es_r.at[d],
            device_id=(c, sib), device_id_type=MESH,
        )

    def share_total(total):
        out_ref[:, out_cols(t)] = total.astype(jnp.bfloat16)
        e_copy(t, 4, xn).start()
        for dy in (2, 1, 3):
            e_copy(t, dy, slot(dy, 0)).start()
        es_copy(t, 0).start()

    def share():
        total = z_sum(xh)
        cross_copy.wait_recv()
        share_total(total + crossing[1].astype(jnp.float32))

    def share_straight():
        @pl.loop(1, 8)
        def _(d):
            s = (c + d) % 8
            pltpu.make_async_remote_copy(
                src_ref=pbuf.at[s], dst_ref=rbuf.at[s], send_sem=d_s.at[s], recv_sem=d_r.at[s],
                device_id=(s, t), device_id_type=MESH,
            ).wait_recv()

        total = rbuf[0].astype(jnp.float32)
        for i in range(1, 8):
            total += rbuf[i].astype(jnp.float32)
        share_total(total)

    def pass_on():
        e_copy(xn, 4, xn).wait_recv()
        for dy in (2, 1, 3):
            e_copy(xn, 4 + dy, slot(dy, 0)).start()
        es_copy(xn, 4).start()

    wide = p % 4 == 0
    first = 3 * p + (p + 7) // 8 + (p + 3) // 8
    ready = jnp.where(q == 0, pick(p, READY[0]), pick(p, READY[1]))

    def h_part(i, n):
        src = pl.ds(pl.multiple_of(q * half + (first + i) * LANES, LANES), n * LANES)
        a = xbuf[:, :, src].reshape(16 * rows, n * LANES)
        r = jnp.dot(st[...], a, preferred_element_type=jnp.float32)
        hs[:, :, pl.ds(i * LANES, n * LANES)] = r.astype(jnp.bfloat16).reshape(8, SLAB_DEV, n * LANES)

    def h1_copy(k, n):
        cols = pl.ds(0, n * LANES)
        return pltpu.make_async_remote_copy(
            src_ref=hs.at[k, :, cols], dst_ref=h1.at[c, :, cols],
            send_sem=h1_s.at[k], recv_sem=h1_r.at[c],
            device_id=(k, t), device_id_type=MESH,
        )

    def h1_wait(s, n):
        cols = pl.ds(0, n * LANES)
        pltpu.make_async_remote_copy(
            src_ref=hs.at[s, :, cols], dst_ref=h1.at[s, :, cols],
            send_sem=h1_s.at[s], recv_sem=h1_r.at[s],
            device_id=(s, t), device_id_type=MESH,
        ).wait_recv()

    def either(f):
        @pl.when(wide)
        def _():
            f(4)

        @pl.when(jnp.logical_not(wide))
        def _():
            f(3)

    def hessian():
        h_part(0, 3)

        @pl.when(wide)
        def _():
            h_part(3, 1)

        h1[c] = hs[c]

        @pl.loop(1, 8)
        def _(d):
            either(lambda n: h1_copy((c + d) % 8, n).start())

    far = (YPX, YMX)
    early = c % 2 == x
    even = (c // 2 - y) % 2 == 0

    @pl.loop(0, NJ - 1)
    def _(i):
        @pl.when(i == 0)
        def _():
            arrive(X2, 0)
            arrive(X2, 1)

        @pl.when(i < NJ - 2)
        def _():
            arrive(X2, i + 2)

        @pl.when(jnp.logical_and(i >= 1, i < NJ - 1))
        def _():
            @pl.when(i == 1)
            def _():
                for j in range(2):
                    got_sib(X2, j)
                    chunk_product((X2,), 5, j)

            got_sib(X2, i + 1)
            chunk_product((X2,), 5, i + 1)

        @pl.when(i == NJ - 2)
        def _():
            send_terms((X2,), 5)

        @pl.when(jnp.logical_and(early, i == CROSS_I))
        def _():
            cross()

        @pl.when(jnp.logical_and(early, i == SHARE_I))
        def _():
            share()

        arrive(YMX, i)
        arrive(YPX, i)

        @pl.when(i > 0)
        def _():
            for kind in far:
                got_sib(kind, i - 1)
            chunk_product(far, 6, i - 1)

        @pl.when(i == SLAB_J + 1)
        def _():
            @pl.loop(0, 4)
            def _(k):
                src = pl.ds(pl.multiple_of(width + k * LANES, LANES), LANES)
                a = xbuf[:, :, src].reshape(16 * rows, LANES).astype(jnp.float32)
                st[pl.ds(pl.multiple_of(k * LANES, LANES), LANES), :] = jnp.transpose(a).astype(jnp.bfloat16)

        @pl.when(i - 1 == ready)
        def _():
            hessian()

    arrive(YMX, NJ - 1)
    for kind in far:
        got_sib(kind, NJ - 2)
    chunk_product(far, 6, NJ - 2)
    for base, kind in ((7, YMX), (6, YPX)):
        if kind == YPX:
            @pl.when(jnp.logical_not(early))
            def _():
                pass_on()

            arrive(YPX, NJ - 1)
        got_sib(kind, NJ - 1)
        chunk_product((kind,), base, NJ - 1)
        send_terms((kind,), base)

    @pl.when(ready >= NJ - 2)
    def _():
        hessian()

    @pl.when(jnp.logical_and(jnp.logical_not(early), even))
    def _():
        share_straight()

    @pl.when(jnp.logical_and(early, even))
    def _():
        pass_on()

    def place(s):
        return 2 * s + q

    def h2_copy(s, n):
        dst = hes_ref.at[:, pl.ds(pl.multiple_of(first * LANES, LANES), n * LANES)]
        return pltpu.make_async_remote_copy(
            src_ref=h1.at[s, :, pl.ds(0, n * LANES)], dst_ref=dst,
            send_sem=h2_s.at[s], recv_sem=h2_r.at[p],
            device_id=(c, place(s)), device_id_type=MESH,
        )

    def h2_wait(s, n):
        f = 3 * s + (s + 7) // 8 + (s + 3) // 8
        dst = hes_ref.at[:, pl.ds(pl.multiple_of(f * LANES, LANES), n * LANES)]
        pltpu.make_async_remote_copy(
            src_ref=h1.at[s, :, pl.ds(0, n * LANES)], dst_ref=dst,
            send_sem=h2_s.at[s], recv_sem=h2_r.at[s],
            device_id=(c, place(s)), device_id_type=MESH,
        ).wait_recv()

    @pl.loop(1, 8)
    def _(d):
        either(lambda n: h1_wait((c + d) % 8, n))

    @pl.loop(1, 8)
    def _(d):
        either(lambda n: h2_copy((p + d) % 8, n).start())

    def keep(n):
        hes_ref[:, pl.ds(pl.multiple_of(first * LANES, LANES), n * LANES)] = h1[p, :, pl.ds(0, n * LANES)]

    either(keep)

    @pl.when(jnp.logical_and(jnp.logical_not(early), jnp.logical_not(even)))
    def _():
        share_straight()

    def own_line():
        for dy in (1, 3, 2):
            s = slot(-dy % 4, 0)
            e_copy(s, dy, xn).wait_recv()
            es_copy(s, dy).start()

    def other_line():
        for dy in (1, 3, 2):
            s = slot(-dy % 4, 1)
            e_copy(s, 4 + dy, xn).wait_recv()
            es_copy(s, 4 + dy).start()

    @pl.when(early)
    def _():
        own_line()

        @pl.when(jnp.logical_not(even))
        def _():
            pass_on()

        other_line()

    @pl.when(jnp.logical_not(early))
    def _():
        other_line()
        own_line()

    for d in range(8):
        s = slot(-(d % 4) % 4, d // 4)
        es_copy(sibling(s), d).wait_recv()

    for s in range(8):
        @pl.when(s != p)
        def _():
            h2_wait(s, 4 if s % 4 == 0 else 3)

    @pl.loop(1, 8)
    def _(d):
        either(lambda n: h1_copy((c + d) % 8, n).wait_send())
        either(lambda n: h2_copy((p + d) % 8, n).wait_send())
        slab_copy(d).wait_send()

    @pl.loop(0, 8)
    def _(k):
        @pl.when(jnp.where(k % 2 == x, k % 4 != z, k != c))
        def _():
            d_copy(k, True).wait_send()

    @pl.when(early)
    def _():
        cross_copy.wait_send()

    for d in range(8):
        es_copy(t, d).wait_send()
        if d:
            e_copy(t, d, sib).wait_send()

    @pl.loop(0, NJ)
    def _(j):
        for kind in range(8):
            if kind != OWN:
                line(kind, j, t, yp).wait_send()
            across(kind, j, t).wait_send()


def fused(tokens_in, codes, group_index, scales):
    rows, width = tokens_in.shape
    dcols = codes.shape[1]
    bf, f32 = jnp.bfloat16, jnp.float32
    dma = pltpu.SemaphoreType.DMA
    table = pltpu.VMEM((512, dcols), bf)
    inputs = (tokens_in, codes, group_index.reshape(width // LANES, LANES), scales)
    return pl.pallas_call(
        kernel,
        name="calibrate",
        out_shape=(
            jax.ShapeDtypeStruct((128, 16 * dcols), bf),
            jax.ShapeDtypeStruct((SLAB_DEV, width // 2), bf),
        ),
        in_specs=[pl.BlockSpec(memory_space=pltpu.HBM)] * 4,
        out_specs=[pl.BlockSpec(memory_space=pltpu.VMEM)] * 2,
        scratch_shapes=[
            pltpu.VMEM((16, rows, NJ * CW), bf),
            pltpu.VMEM((width, dcols), bf),
            pltpu.VMEM((width, dcols), jnp.int32),
            pltpu.VMEM((width // LANES, LANES), jnp.int32),
            pltpu.VMEM(scales.shape, f32),
            table, table, table,
            pltpu.VMEM((BLK, 512), bf),
            pltpu.VMEM((8, 2 * rows, dcols), bf),
            pltpu.VMEM((8, 2 * rows, dcols), bf),
            pltpu.VMEM((8, rows, LANES), bf),
            pltpu.VMEM((512, 16 * rows), bf),
            pltpu.VMEM((8, SLAB_DEV, 512), bf),
            pltpu.VMEM((8, SLAB_DEV, 512), bf),
            pltpu.VMEM((8, 2 * rows, dcols), f32),
            dma((4,)), dma((width // BLK,)),
            dma((8, NJ)), dma((8, NJ)), dma((8, NJ)), dma((8, NJ)),
            dma((8,)), dma((8,)), dma((8,)), dma((8,)),
            dma((8,)), dma((8,)), dma((8,)), dma((8,)),
            dma((8,)), dma((8,)), dma((8,)), dma((8,)),
            pltpu.VMEM((2, 2 * rows, dcols), bf), dma, dma,
        ],
        compiler_params=pltpu.CompilerParams(
            collective_id=0, has_side_effects=True, vmem_limit_bytes=46 << 20
        ),
        cost_estimate=pl.CostEstimate(
            flops=16 * 10**9, bytes_accessed=20 * 10**6, transcendentals=0
        ),
    )(*(pltpu.with_memory_space_constraint(v, pltpu.HBM) for v in inputs))


def local(tokens_in, codes, group_index, scales):
    total_tokens = tokens_in.shape[0] * lax.axis_size("tok")
    next_input, hessian = fused(tokens_in, codes, group_index, scales)
    return hessian.astype(jnp.float32) * (2.0 / total_tokens), next_input


def solution(mesh):
    return jax.shard_map(
        local,
        mesh=mesh,
        in_specs=(P("tok", "col"), P("col", "tok"), P("col"), P(None, "tok")),
        out_specs=(P("col", "tok"), P("col", None)),
        check_vma=False,
    )
```
